32 devices in a mesh: patch: 8 (over z, x), visit: 4 (over y, core).
Axes of the slice: x: 2, y: 2, z: 4, core: 2. Of those that a mesh axis runs over, the one named last changes fastest.
Arguments:
- template: bfloat16 [8, 1024, 2048], P('patch', 'visit'), may hold values from -40 to 40
- blocks: bfloat16 [1024, 16, 2048], P(('patch', 'visit')), may hold values from -80 to 80
- dest: int32 [1024], P(('patch', 'visit')), may hold values from 0 to 31, as said below
- offset: int32 [1024], P(('patch', 'visit')), may hold values from 0 to 240
- visit_id: int32 [1024], P(('patch', 'visit')), may hold values from 0 to 1
- badmask: int32 [1024, 16], P(('patch', 'visit')), may hold values from 0 to 65535, as said below
Outputs:
- difference: bfloat16 [2, 8, 1024, 2048], P(None, 'patch', 'visit')
- coeffs: float32 [2, 8, 29], P(None, 'patch')
The draws below stay inside these ranges and needn't reach their ends.
Inputs may be any that keep to these rules, and one draw needn't show every extreme that they name: dest counts devices along patch+visit; of one device's 32 blocks at most 2 go to one device, and one device receives exactly 2 blocks from every device. Bit q of badmask[n, r] flags row r of block n, column group q, as bad.
All inputs are finite; a program needn't handle non-finite values.
Results may differ from the reference program's by a relative error of at most 0.0078.
Values may be sent and summed in bfloat16 or wider, within the bound.
No kernel may reach another device: no remote copies, remote signals or barrier semaphores. Data moves between devices by JAX's collectives and lax.ppermute only.
A program may use at most 256 MiB of HBM per device.

```python
import math
import jax
import jax.numpy as jnp
import numpy as np
from jax import lax

ROWS_DEV = 256
COLUMNS = 2048
BLOCK_ROWS = 16
SLOT_CAP = 2
HALF_TAPS = 10
DEGREE = 6
VISITS = 2
BASIS_COUNT = 28
TERMS = 29
PATCHES = 8
PH = 1024
SOURCES = 32
BLOCKS_DEV = 32
BLOCKS = 1024
N_VISIT = 4


def route_targets(key):
    base_key = jax.random.fold_in(key, 11)
    key_hot, key_arc, key_pick, key_order = jax.random.split(base_key, 4)
    hot_device = jax.random.randint(key_hot, (), 0, SOURCES, dtype=jnp.int32)
    arc_length = (BLOCKS_DEV - SLOT_CAP) // 2
    free_length = BLOCKS_DEV - SLOT_CAP - arc_length
    arc_shift = jax.random.randint(key_arc, (), 0, SOURCES - 1, dtype=jnp.int32)
    source_pos = jnp.arange(SOURCES, dtype=jnp.int32)
    arc_pos = (source_pos[:, None] * arc_length + arc_shift + jnp.arange(arc_length, dtype=jnp.int32)[None, :]) % (SOURCES - 1)

    def pick_others(subkey):
        return jax.random.permutation(subkey, SOURCES - 1)[:free_length].astype(jnp.int32)
    picked = jax.vmap(pick_others)(jax.random.split(key_pick, SOURCES))
    others = jnp.concatenate([arc_pos, picked], axis=1)
    hot_part = jnp.zeros((SOURCES, SLOT_CAP), jnp.int32) + hot_device
    targets = jnp.concatenate([hot_part, (hot_device + 1 + others) % SOURCES], axis=1)

    def reorder(subkey, target_row):
        return target_row[jax.random.permutation(subkey, BLOCKS_DEV)]
    shuffled = jax.vmap(reorder)(jax.random.split(key_order, SOURCES), targets)
    return shuffled.reshape(-1).astype(jnp.int32)


def offsets_of(key):
    return jax.random.randint(jax.random.fold_in(key, 12), (BLOCKS,), 0, ROWS_DEV - BLOCK_ROWS + 1, dtype=jnp.int32)


def visits_of(key):
    return jax.random.randint(jax.random.fold_in(key, 13), (BLOCKS,), 0, VISITS, dtype=jnp.int32)


def template_field(key):
    base_key = jax.random.fold_in(key, 15)
    key_base, key_row, key_col = jax.random.split(base_key, 3)
    full_shape = (PATCHES, PH, COLUMNS)
    growth = jnp.arange(PH, dtype=jnp.float32) / PH
    row_scale = 3.0 ** growth[None, :, None] * jnp.exp(jax.random.uniform(key_row, (PATCHES, PH, 1), jnp.float32, 0.0, math.log(3.3)))
    col_scale = jnp.exp(jax.random.uniform(key_col, (PATCHES, 1, COLUMNS), jnp.float32, 0.0, math.log(2.0)))
    noise_part = jnp.clip(jax.random.normal(key_base, full_shape, jnp.float32), -5.0, 5.0)
    return 0.4 * noise_part * row_scale * col_scale


def draw_template(key, part):
    return template_field(key).astype(jnp.bfloat16)


def draw_dest(key, part):
    return route_targets(key)


def draw_offset(key, part):
    return offsets_of(key)


def draw_visit_id(key, part):
    return visits_of(key)


def draw_badmask(key, part):
    word_keys = jax.random.split(jax.random.fold_in(key, 14), 7)
    word_shape = (BLOCKS, BLOCK_ROWS)
    merged = jnp.zeros(word_shape, jnp.int32)
    for word_pos in range(7):
        fresh = jax.random.randint(word_keys[word_pos], word_shape, 0, 65536, dtype=jnp.int32)
        merged = jnp.bitwise_or(merged, fresh)
    return merged


def right_neighbour(rows):
    return jnp.concatenate([rows[:, :, 1:], jnp.zeros_like(rows[:, :, :1])], axis=2)


def draw_blocks(key, part):
    targets = route_targets(key)
    rows_off = offsets_of(key)
    visit_of = visits_of(key)
    field = template_field(key)
    bands = PH // ROWS_DEV
    patch_of = targets // bands
    first_row = targets % bands * ROWS_DEV + rows_off
    row_index = first_row[:, None] + jnp.arange(BLOCK_ROWS, dtype=jnp.int32)[None, :]
    gathered = field[patch_of[:, None], row_index]
    next_index = jnp.minimum(row_index + 1, PH - 1)
    inside = (row_index + 1 < PH).astype(jnp.float32)
    below = field[patch_of[:, None], next_index] * inside[:, :, None]
    row_frac = jax.random.uniform(jax.random.fold_in(key, 19), (PATCHES, VISITS), jnp.float32, 0.25, 0.45)
    col_frac = jax.random.uniform(jax.random.fold_in(key, 20), (PATCHES, VISITS), jnp.float32, 0.25, 0.45)
    row_weight = row_frac[patch_of, visit_of][:, None, None]
    col_weight = col_frac[patch_of, visit_of][:, None, None]
    vertical = (1.0 - row_weight) * gathered + row_weight * below
    shifted = (1.0 - col_weight) * vertical + col_weight * right_neighbour(vertical)
    gains = jax.random.uniform(jax.random.fold_in(key, 16), (PATCHES, VISITS), jnp.float32, 0.7, 1.3)
    skies = jax.random.uniform(jax.random.fold_in(key, 17), (PATCHES, VISITS), jnp.float32, 0.5, 2.0)
    slope = gains[patch_of, visit_of][:, None] * (0.6 + 0.8 * row_index.astype(jnp.float32) / PH)
    sky_level = skies[patch_of, visit_of][:, None, None]
    block_shape = (BLOCKS, BLOCK_ROWS, COLUMNS)
    noise_part = 0.3 * jnp.clip(jax.random.normal(jax.random.fold_in(key, 18), block_shape, jnp.float32), -5.0, 5.0)
    return (slope[:, :, None] * shifted + sky_level + noise_part).astype(jnp.bfloat16)


def setup_inputs(seed: int = 0) -> dict:
    key_list = jax.random.split(jax.random.key(seed), 7)
    return {
        "template": draw_template(jax.random.fold_in(key_list[6], 71), 0),
        "blocks": draw_blocks(jax.random.fold_in(key_list[6], 71), 0),
        "dest": draw_dest(jax.random.fold_in(key_list[6], 71), 0),
        "offset": draw_offset(jax.random.fold_in(key_list[6], 71), 0),
        "visit_id": draw_visit_id(jax.random.fold_in(key_list[6], 71), 0),
        "badmask": draw_badmask(jax.random.fold_in(key_list[6], 71), 0),
    }


sigma_taps = 2.0

def taps_table():
    places = np.arange(-HALF_TAPS, HALF_TAPS + 1) * 1.0
    basis_rows = []
    for exponent in range(DEGREE + 1):
        vector = places ** exponent * np.exp(-places ** 2 / (2.0 * sigma_taps ** 2))
        for earlier in basis_rows:
            vector = vector - np.dot(earlier, vector) * earlier
        vector = vector / np.sqrt(np.dot(vector, vector))
        basis_rows.append(vector)
    return np.stack(basis_rows).astype(np.float32)

def pair_table():
    selector = np.zeros(((DEGREE + 1) * (DEGREE + 2) // 2, DEGREE + 1, DEGREE + 1), np.float32)
    position = 0
    for column_power in range(DEGREE + 1):
        for row_power in range(DEGREE + 1 - column_power):
            selector[position, column_power, row_power] = 1.0
            position += 1
    return selector

def solve_normal(matrix, vector_rhs):
    lower_factor = jnp.linalg.cholesky(matrix)
    middle = jax.scipy.linalg.solve_triangular(lower_factor, vector_rhs, lower=True)
    return jax.scipy.linalg.solve_triangular(lower_factor, middle, lower=True, trans=1)

def kernel_taps(coeff_rows, taps_f32):
    selector = jnp.asarray(pair_table())
    nbasis = selector.shape[0]
    per_column = jnp.einsum('vb,bji->vji', coeff_rows[:, :nbasis], selector, precision=lax.Precision.HIGHEST)
    return jnp.einsum('vji,ik->vjk', per_column, taps_f32, precision=lax.Precision.HIGHEST).astype(jnp.bfloat16)

def reference(template, blocks, dest, offset, visit_id, badmask):
    taps_f32 = jnp.asarray(taps_table()).astype(jnp.bfloat16).astype(jnp.float32)
    ntaps = 2 * HALF_TAPS + 1
    patch_of = dest // N_VISIT
    within = dest % N_VISIT * ROWS_DEV + offset
    frame_start = (patch_of * VISITS + visit_id) * PH + within
    row_target = (frame_start[:, None] + jnp.arange(BLOCK_ROWS, dtype=jnp.int32)[None, :]).reshape(-1)
    shift_table = jnp.arange(16, dtype=jnp.int32)[None, None, :]
    good_flag = (1 - jnp.bitwise_and(jnp.right_shift(badmask[:, :, None], shift_table), 1)).astype(jnp.float32)
    values = blocks.astype(jnp.float32).reshape(BLOCKS, BLOCK_ROWS, 16, COLUMNS // 16) * good_flag[..., None]
    frame_rows = PATCHES * VISITS * PH
    summed = jnp.zeros((frame_rows, COLUMNS), jnp.float32).at[row_target].add(values.reshape(-1, COLUMNS))
    counted = jnp.zeros((frame_rows, 16), jnp.float32).at[row_target].add(good_flag.reshape(-1, 16))

    def one_patch(item):
        patch_tile, summed_patch, counted_patch = item
        spread = jnp.repeat(counted_patch, COLUMNS // 16, axis=2)
        science = (summed_patch / jnp.maximum(spread, 1.0)).astype(jnp.bfloat16)
        weight = jnp.minimum(spread, 1.0).astype(jnp.bfloat16)
        padded = jnp.pad(patch_tile.astype(jnp.float32), HALF_TAPS)
        column_conv = []
        for column_power in range(DEGREE + 1):
            accum = jnp.zeros((PH + 2 * HALF_TAPS, COLUMNS), jnp.float32)
            for shift_pos in range(ntaps):
                accum = accum + taps_f32[column_power, shift_pos] * padded[:, shift_pos:shift_pos + COLUMNS]
            column_conv.append(accum.astype(jnp.bfloat16).astype(jnp.float32))
        basis_list = []
        for column_power in range(DEGREE + 1):
            for row_power in range(DEGREE + 1 - column_power):
                accum = jnp.zeros((PH, COLUMNS), jnp.float32)
                for shift_pos in range(ntaps):
                    accum = accum + taps_f32[row_power, shift_pos] * column_conv[column_power][shift_pos:shift_pos + PH]
                basis_list.append(accum.astype(jnp.bfloat16))
        design = jnp.stack(basis_list + [jnp.ones((PH, COLUMNS), jnp.bfloat16)]).reshape(TERMS, PH * COLUMNS)
        design_t = design.T
        solved = []
        for visit_pos in range(VISITS):
            weighted = design * weight[visit_pos].reshape(1, -1)
            matrix = jnp.dot(weighted.astype(jnp.float32), design_t.astype(jnp.float32), preferred_element_type=jnp.float32)
            vector_rhs = jnp.dot(weighted.astype(jnp.float32), science[visit_pos].reshape(-1).astype(jnp.float32), preferred_element_type=jnp.float32)
            solved.append(solve_normal(matrix, vector_rhs))
        coeff_rows = jnp.stack(solved)
        kernel_rows = kernel_taps(coeff_rows, taps_f32).astype(jnp.float32)
        diffs = []
        for visit_pos in range(VISITS):
            model = jnp.zeros((PH, COLUMNS), jnp.float32) + coeff_rows[visit_pos, BASIS_COUNT]
            for column_power in range(DEGREE + 1):
                for shift_pos in range(ntaps):
                    model = model + kernel_rows[visit_pos, column_power, shift_pos] * column_conv[column_power][shift_pos:shift_pos + PH]
            diffs.append((weight[visit_pos].astype(jnp.float32) * (science[visit_pos].astype(jnp.float32) - model)).astype(jnp.bfloat16))
        return (jnp.stack(diffs), coeff_rows)
    summed_four = summed.reshape(PATCHES, VISITS, PH, COLUMNS)
    counted_four = counted.reshape(PATCHES, VISITS, PH, 16)
    diffs, coeff_all = lax.map(one_patch, (template, summed_four, counted_four))
    return (jnp.transpose(diffs, (1, 0, 2, 3)), jnp.transpose(coeff_all, (1, 0, 2)))
```

```python
import jax
import jax.numpy as jnp
import ml_dtypes
import numpy as np
from jax import lax
from jax.experimental import pallas as pl
from jax.experimental.pallas import tpu as pltpu
from jax.sharding import PartitionSpec as P

BLOCK_ROWS = 16
SLOT_CAP = 2
HALF_TAPS = 10
NTAPS = 2 * HALF_TAPS + 1
DEGREE = 6
NPOW = DEGREE + 1
VISITS = 2
BASIS_COUNT = 28
TERMS = 29
GROUPS = 16
TILE = 64
SPAN = 96
SIGMA = 2.0
MIB = 1 << 20


def taps_table():
    places = np.arange(-HALF_TAPS, HALF_TAPS + 1) * 1.0
    basis_rows = []
    for exponent in range(NPOW):
        vector = places**exponent * np.exp(-(places**2) / (2.0 * SIGMA**2))
        for earlier in basis_rows:
            vector = vector - np.dot(earlier, vector) * earlier
        vector = vector / np.sqrt(np.dot(vector, vector))
        basis_rows.append(vector)
    table = np.stack(basis_rows).astype(np.float32)
    return table.astype(ml_dtypes.bfloat16).astype(np.float32)


def band(taps_row, count_out, count_in):
    out = np.zeros((count_out, count_in), np.float32)
    for row in range(count_out):
        out[row, row : row + NTAPS] = taps_row
    return out


def column_table(taps):
    return np.concatenate([band(taps[j], 128, 256).T for j in range(NPOW)], axis=1)


def row_table(taps):
    bands = np.stack([band(taps[i], TILE, SPAN) for i in range(NPOW)])
    bands = bands.reshape(NPOW, TILE // 8, 8, SPAN)
    pieces = []
    for j in range(NPOW):
        pieces.append(bands[: NPOW - j].transpose(1, 0, 2, 3).reshape(-1, SPAN))
    return np.concatenate(pieces, axis=0)


def place_table():
    out = np.zeros((TERMS, 8, 128), np.float32)
    index = 0
    for j in range(NPOW):
        for i in range(NPOW - j):
            out[index, i, j] = 1.0
            index += 1
    out[BASIS_COUNT, 7, 0] = 1.0
    return out


def params(mib):
    return pltpu.CompilerParams(vmem_limit_bytes=mib * MIB)


def pack_kernel(dest, offset, visit, bad_s, bad_v, blocks, send, meta, buf, out, zero, cnt, sem_in, sem_out, row_count):
    count = blocks.shape[0]
    cols = blocks.shape[2]
    slots = send.shape[0]
    group = min(8, count)
    for k in range(count // group):
        part = pl.ds(k * group, group)
        pltpu.make_async_copy(blocks.at[part], buf.at[part], sem_in.at[k]).start()
    zero[...] = jnp.zeros_like(zero)

    def clear(d, carry):
        cnt[d] = 0
        return carry

    lax.fori_loop(0, slots // SLOT_CAP, clear, 0)
    flags = jnp.transpose(bad_v[...])
    for k in range(count // group):
        part = pl.ds(k * group, group)
        pltpu.make_async_copy(blocks.at[part], buf.at[part], sem_in.at[k]).wait()
        for n in range(k * group, (k + 1) * group):
            word = jnp.broadcast_to(flags[:, n : n + 1], (BLOCK_ROWS, 128))
            for q in range(GROUPS):
                lanes = slice(q * (cols // GROUPS), (q + 1) * (cols // GROUPS))
                good = (1 - jnp.bitwise_and(jnp.right_shift(word, q), 1)).astype(jnp.float32)
                out[n, :, lanes] = buf[n, :, lanes] * good.astype(jnp.bfloat16)
            d = dest[n]
            rank = cnt[d]
            cnt[d] = rank + 1
            pltpu.make_async_copy(out.at[n], send.at[d * SLOT_CAP + rank], sem_out).start()

    def fill(d, carry):
        for r in range(SLOT_CAP):

            @pl.when(cnt[d] <= r)
            def _():
                pltpu.make_async_copy(zero, send.at[d * SLOT_CAP + r], sem_out).start()
                meta[d * SLOT_CAP + r, 0] = -1

        cnt[d] = 0
        return carry

    lax.fori_loop(0, slots // SLOT_CAP, fill, 0)

    def describe(n, carry):
        d = dest[n]
        rank = cnt[d]
        cnt[d] = rank + 1
        slot = d * SLOT_CAP + rank
        meta[slot, 0] = visit[n] * row_count + offset[n]
        for r in range(BLOCK_ROWS):
            meta[slot, 1 + r] = bad_s[n, r]
        return carry

    lax.fori_loop(0, count, describe, 0)
    pltpu.make_async_copy(send, send, sem_out).wait()


def pack(dest, offset, visit_id, badmask, blocks, slots, row_count):
    count, _, cols = blocks.shape
    smem = pl.BlockSpec(memory_space=pltpu.SMEM)
    hbm = pl.BlockSpec(memory_space=pl.ANY)

    def kernel(*refs):
        pack_kernel(*refs, row_count=row_count)

    return pl.pallas_call(
        kernel,
        out_shape=(
            jax.ShapeDtypeStruct((slots, BLOCK_ROWS, cols), jnp.bfloat16),
            jax.ShapeDtypeStruct((slots, 1 + BLOCK_ROWS), jnp.int32),
        ),
        in_specs=[smem, smem, smem, smem, pl.BlockSpec(memory_space=pltpu.VMEM), hbm],
        out_specs=(hbm, smem),
        scratch_shapes=[
            pltpu.VMEM((count, BLOCK_ROWS, cols), jnp.bfloat16),
            pltpu.VMEM((count, BLOCK_ROWS, cols), jnp.bfloat16),
            pltpu.VMEM((BLOCK_ROWS, cols), jnp.bfloat16),
            pltpu.SMEM((slots // SLOT_CAP,), jnp.int32),
            pltpu.SemaphoreType.DMA((max(1, count // 8),)),
            pltpu.SemaphoreType.DMA,
        ],
        compiler_params=params(40),
        name="pack_blocks",
    )(dest, offset, visit_id, badmask, badmask, blocks)


def column_kernel(padded, table, out):
    chunk = out.shape[2]
    base = pl.program_id(0) * chunk
    for k in range(chunk // 128):
        start = pl.multiple_of(base + k * 128, 128)
        window = padded[:, pl.ds(start, 256)]
        result = jnp.dot(window, table[...], preferred_element_type=jnp.float32)
        for j in range(NPOW):
            out[j, :, k * 128 : (k + 1) * 128] = result[:, j * 128 : (j + 1) * 128].astype(jnp.bfloat16)


def column_pass(padded, taps, cols):
    rows = padded.shape[0]
    chunk = 512
    table = jnp.asarray(column_table(taps).astype(ml_dtypes.bfloat16))
    return pl.pallas_call(
        column_kernel,
        grid=(cols // chunk,),
        out_shape=jax.ShapeDtypeStruct((NPOW, rows, cols), jnp.bfloat16),
        in_specs=[
            pl.BlockSpec(padded.shape, lambda c: (0, 0)),
            pl.BlockSpec(table.shape, lambda c: (0, 0)),
        ],
        out_specs=pl.BlockSpec((NPOW, rows, chunk), lambda c: (0, 0, c)),
        compiler_params=params(24),
        name="column_pass",
    )(padded, table)


GRAM_ROWS = 240


def gram_kernel(images, table, weight, out, stage):
    cols = images.shape[2]
    chunk = 1024
    step = pl.program_id(0)

    @pl.when(step == 0)
    def _():
        out[...] = jnp.zeros_like(out)

    first = pl.multiple_of(step * TILE, TILE)
    ones = jnp.ones((8, chunk), jnp.float32)
    blank = jnp.zeros((8, chunk), jnp.float32)
    for k in range(cols // chunk):
        lanes = slice(k * chunk, (k + 1) * chunk)
        at = 0
        for j in range(NPOW):
            size = TILE * (NPOW - j)
            window = images[j, pl.ds(first, SPAN), lanes]
            stage[at : at + size, :] = jnp.dot(
                table[at : at + size, :], window, preferred_element_type=jnp.float32
            )
            at += size
        for cb in range(TILE // 8):
            pieces = []
            at = 0
            for j in range(NPOW):
                size = 8 * (NPOW - j)
                pieces.append(stage[at + cb * size : at + (cb + 1) * size, :])
                at += TILE * (NPOW - j)
            basis = jnp.concatenate(pieces + [ones, blank], axis=0)
            scaled = []
            for v in range(VISITS):
                w = weight[v, cb * 8 : (cb + 1) * 8, lanes]
                scaled.append(
                    (basis.reshape(GRAM_ROWS // 8, 8, chunk) * w[None]).reshape(GRAM_ROWS, chunk).astype(jnp.bfloat16)
                )
            out[...] += lax.dot_general(
                jnp.concatenate(scaled, axis=0),
                basis.astype(jnp.bfloat16),
                (((1,), (1,)), ((), ())),
                preferred_element_type=jnp.float32,
            )


def gram(images, weight, taps):
    rows = weight.shape[1]
    cols = weight.shape[2]
    table = jnp.asarray(row_table(taps).astype(ml_dtypes.bfloat16))
    acc = pl.pallas_call(
        gram_kernel,
        grid=(rows // TILE,),
        out_shape=jax.ShapeDtypeStruct((VISITS * GRAM_ROWS, GRAM_ROWS), jnp.float32),
        in_specs=[
            pl.BlockSpec(images.shape, lambda t: (0, 0, 0)),
            pl.BlockSpec(table.shape, lambda t: (0, 0)),
            pl.BlockSpec((VISITS, TILE, cols), lambda t: (0, t, 0)),
        ],
        out_specs=pl.BlockSpec((VISITS * GRAM_ROWS, GRAM_ROWS), lambda t: (0, 0)),
        scratch_shapes=[pltpu.VMEM((BASIS_COUNT * TILE, 1024), jnp.float32)],
        compiler_params=params(48),
        name="gram",
    )(images, table, weight)
    blocks = acc.reshape(VISITS, GRAM_ROWS // 8, 8, GRAM_ROWS // 8, 8)
    same = jnp.asarray(np.eye(8, dtype=np.float32))[None, None, :, None, :]
    return jnp.sum(blocks * same, axis=(2, 4))[:, :TERMS, :TERMS]


def place_kernel(got, placing, count, images, table, science, sums, acc, total):
    step = pl.program_id(0)
    rows = science.shape[1]

    @pl.when(step == 0)
    def _():
        acc[...] = jnp.zeros_like(acc)
        total[...] = jnp.zeros_like(total)

    chunk = science.shape[2]
    summed = jnp.dot(placing[...], got[...].reshape(-1, chunk), preferred_element_type=jnp.float32)
    spread = count[...].astype(jnp.float32)
    value = (summed / jnp.maximum(spread, 1.0)).astype(jnp.bfloat16)
    science[...] = value.reshape(science.shape)
    weighted = value * jnp.minimum(spread, 1.0).astype(jnp.bfloat16)
    for v in range(VISITS):
        part = weighted[v * rows : (v + 1) * rows, :].astype(jnp.float32)
        fold = jnp.sum(part.reshape(rows // 8, 8, chunk), axis=0)
        total[v * 8 : (v + 1) * 8, :] += sum(fold[:, k * 128 : (k + 1) * 128] for k in range(chunk // 128))
    partial = None
    for t in range(rows // TILE):
        left = jnp.concatenate(
            [weighted[v * rows + t * TILE : v * rows + (t + 1) * TILE, :] for v in range(VISITS)], axis=0
        )
        right = images[:, t * TILE : t * TILE + SPAN, :].reshape(NPOW * SPAN, chunk)
        product = lax.dot_general(left, right, (((1,), (1,)), ((), ())), preferred_element_type=jnp.float32)
        partial = product if partial is None else partial + product
    acc[...] += partial

    @pl.when(step == pl.num_programs(0) - 1)
    def _():
        row_id = lax.broadcasted_iota(jnp.int32, (16, 128), 0)
        lane_id = lax.broadcasted_iota(jnp.int32, (16, 128), 1)
        result = jnp.zeros((16, 128), jnp.float32)
        for v in range(VISITS):
            for j in range(NPOW):
                cross = acc[v * TILE : (v + 1) * TILE, j * SPAN : (j + 1) * SPAN]
                for i in range(NPOW - j):
                    item = jnp.sum(cross * table[i], axis=0, keepdims=True)
                    item = jnp.sum(item, axis=1, keepdims=True)
                    result += jnp.where((row_id == v * 8 + i) & (lane_id == j), item, 0.0)
            item = jnp.sum(total[v * 8 : (v + 1) * 8, :], axis=0, keepdims=True)
            item = jnp.sum(item, axis=1, keepdims=True)
            result += jnp.where((row_id == v * 8 + 7) & (lane_id == 0), item, 0.0)
        sums[...] = result


def place(got, placing, count, images, bands, row_count):
    slots, _, cols = got.shape
    chunk = 256
    return pl.pallas_call(
        place_kernel,
        grid=(cols // chunk,),
        out_shape=(
            jax.ShapeDtypeStruct((VISITS, row_count, cols), jnp.bfloat16),
            jax.ShapeDtypeStruct((16, 128), jnp.float32),
        ),
        in_specs=[
            pl.BlockSpec((slots, BLOCK_ROWS, chunk), lambda c: (0, 0, c)),
            pl.BlockSpec(placing.shape, lambda c: (0, 0)),
            pl.BlockSpec((VISITS * row_count, chunk), lambda c: (0, c)),
            pl.BlockSpec((NPOW, images.shape[1], chunk), lambda c: (0, 0, c)),
            pl.BlockSpec(bands.shape, lambda c: (0, 0, 0)),
        ],
        out_specs=(
            pl.BlockSpec((VISITS, row_count, chunk), lambda c: (0, 0, c)),
            pl.BlockSpec((16, 128), lambda c: (0, 0)),
        ),
        scratch_shapes=[
            pltpu.VMEM((VISITS * TILE, NPOW * SPAN), jnp.float32),
            pltpu.VMEM((16, 128), jnp.float32),
        ],
        compiler_params=params(40),
        name="place_and_correlate",
    )(got, placing, count, images, bands)


def model_kernel(sums, inverse, table, images, science, count, out, coeffs, wide, narrow, level):
    step = pl.program_id(0)
    rows = science.shape[1]
    chunk = science.shape[2]

    @pl.when(step == 0)
    def _():
        rhs = sums[0:16, :]
        for k in range(1, sums.shape[0] // 16):
            rhs = rhs + sums[k * 16 : (k + 1) * 16, :]
        row_id = lax.broadcasted_iota(jnp.int32, (32, 128), 0)
        lane_id = lax.broadcasted_iota(jnp.int32, (32, 128), 1)
        for v in range(VISITS):
            product = inverse[v] * rhs[v * 8 : (v + 1) * 8, :][None]
            column = jnp.sum(jnp.sum(product, axis=1), axis=1, keepdims=True)
            row = jnp.sum(jnp.where(row_id == lane_id, column, 0.0), axis=0, keepdims=True)
            coeffs[v : v + 1, :] = row[:, :TERMS]
            level[v * 8 : (v + 1) * 8, :] = jnp.broadcast_to(column[BASIS_COUNT : BASIS_COUNT + 1, :], (8, 128))
            index = 0
            for j in range(NPOW):
                kernel = jnp.zeros((TILE, SPAN), jnp.float32)
                for i in range(NPOW - j):
                    kernel = kernel + column[index : index + 1, :] * table[i]
                    index += 1
                wide[v * TILE : (v + 1) * TILE, j * SPAN : (j + 1) * SPAN] = kernel
        narrow[...] = wide[...].astype(jnp.bfloat16)

    for t in range(rows // TILE):
        right = images[:, t * TILE : t * TILE + SPAN, :].reshape(NPOW * SPAN, chunk)
        model = jnp.dot(narrow[...], right, preferred_element_type=jnp.float32)
        for v in range(VISITS):
            at = slice(t * TILE, (t + 1) * TILE)
            full = model[v * TILE : (v + 1) * TILE, :] + level[v * 8 : v * 8 + 1, 0:1]
            weight = jnp.minimum(count[v, at, :].astype(jnp.float32), 1.0)
            out[v, at, :] = (weight * (science[v, at, :].astype(jnp.float32) - full)).astype(jnp.bfloat16)


def model(sums, inverse, images, science, count, bands):
    _, rows, cols = science.shape
    chunk = 256
    return pl.pallas_call(
        model_kernel,
        grid=(cols // chunk,),
        out_shape=(
            jax.ShapeDtypeStruct((VISITS, rows, cols), jnp.bfloat16),
            jax.ShapeDtypeStruct((VISITS, TERMS), jnp.float32),
        ),
        in_specs=[
            pl.BlockSpec(sums.shape, lambda c: (0, 0)),
            pl.BlockSpec(inverse.shape, lambda c: (0, 0, 0, 0)),
            pl.BlockSpec(bands.shape, lambda c: (0, 0, 0)),
            pl.BlockSpec((NPOW, images.shape[1], chunk), lambda c: (0, 0, c)),
            pl.BlockSpec((VISITS, rows, chunk), lambda c: (0, 0, c)),
            pl.BlockSpec((VISITS, rows, chunk), lambda c: (0, 0, c)),
        ],
        out_specs=(
            pl.BlockSpec((VISITS, rows, chunk), lambda c: (0, 0, c)),
            pl.BlockSpec((VISITS, TERMS), lambda c: (0, 0)),
        ),
        scratch_shapes=[
            pltpu.VMEM((VISITS * TILE, NPOW * SPAN), jnp.float32),
            pltpu.VMEM((VISITS * TILE, NPOW * SPAN), jnp.bfloat16),
            pltpu.VMEM((16, 128), jnp.float32),
        ],
        compiler_params=params(40),
        name="model_and_difference",
    )(sums, inverse, bands, images, science, count)


def inverse_of(matrix):
    eye = jnp.broadcast_to(jnp.eye(TERMS, dtype=jnp.float32), matrix.shape)
    lower = jnp.linalg.cholesky(matrix)
    half = jax.scipy.linalg.solve_triangular(lower, eye, lower=True)
    return jnp.einsum("vkb,vkc->vbc", half, half, precision=lax.Precision.HIGHEST)


def halo(rows):
    count = lax.axis_size("visit")
    up = [(i, i + 1) for i in range(count - 1)]
    down = [(i + 1, i) for i in range(count - 1)]
    above = lax.ppermute(rows[-HALF_TAPS:], "visit", up)
    below = lax.ppermute(rows[:HALF_TAPS], "visit", down)
    return above, below


def coverage(got_meta, row_count):
    slots = got_meta.shape[0]
    start = got_meta[:, 0]
    words = got_meta[:, 1:]
    shifts = jnp.arange(GROUPS, dtype=jnp.int32)[None, None, :]
    bad = jnp.bitwise_and(jnp.right_shift(words[:, :, None], shifts), 1)
    good = (1 - bad).astype(jnp.bfloat16).reshape(slots * BLOCK_ROWS, GROUPS)
    target = jnp.where(
        start[:, None] >= 0,
        start[:, None] + jnp.arange(BLOCK_ROWS, dtype=jnp.int32)[None, :],
        -1,
    ).reshape(-1)
    placing = (jnp.arange(VISITS * row_count, dtype=jnp.int32)[:, None] == target[None, :]).astype(jnp.bfloat16)
    counted = jnp.dot(placing, good, preferred_element_type=jnp.float32)
    return placing, counted


def body(template, blocks, dest, offset, visit_id, badmask):
    row_count = template.shape[1]
    cols = template.shape[2]
    axes = ("patch", "visit")
    sources = lax.axis_size("patch") * lax.axis_size("visit")
    slots = sources * SLOT_CAP
    taps = taps_table()
    bands = jnp.asarray(np.stack([band(taps[i], TILE, SPAN) for i in range(NPOW)]))

    send, meta = pack(dest, offset, visit_id, badmask, blocks, slots, row_count)
    got = lax.all_to_all(send, axes, split_axis=0, concat_axis=0, tiled=True)

    above, below = halo(template[0])
    stored = row_count - TILE + SPAN
    tail = stored - row_count - 2 * HALF_TAPS
    tall = jnp.concatenate([above, template[0], below, jnp.zeros((tail, cols), jnp.bfloat16)], axis=0)
    padded = jnp.pad(tall, ((0, 0), (HALF_TAPS, 128 - HALF_TAPS)))
    images = column_pass(padded, taps, cols)

    meta, images = lax.optimization_barrier((meta, images))
    got_meta = lax.all_to_all(meta, axes, split_axis=0, concat_axis=0, tiled=True)
    placing, counted = coverage(got_meta, row_count)
    spread = jnp.repeat(counted, cols // GROUPS, axis=1)
    weight = jnp.minimum(spread, 1.0).reshape(VISITS, row_count, cols)
    count = spread.astype(jnp.bfloat16)

    normal = lax.psum(gram(images, weight, taps), "visit")
    inverse = jnp.einsum(
        "vcb,bij->vcij", inverse_of(normal), jnp.asarray(place_table()), precision=lax.Precision.HIGHEST
    )
    inverse = jnp.pad(inverse, ((0, 0), (0, 32 - TERMS), (0, 0), (0, 0)))

    science, sums = place(got, placing, count, images, bands, row_count)
    sums = lax.all_gather(sums, "visit", axis=0, tiled=True)
    difference, coeffs = model(sums, inverse, images, science, count.reshape(VISITS, row_count, cols), bands)
    return (difference[:, None], coeffs[:, None])


def solution(mesh):
    in_specs = (
        P("patch", "visit", None),
        P(("patch", "visit"), None, None),
        P(("patch", "visit")),
        P(("patch", "visit")),
        P(("patch", "visit")),
        P(("patch", "visit"), None),
    )
    out_specs = (P(None, "patch", "visit", None), P(None, "patch", None))
    return jax.shard_map(body, mesh=mesh, in_specs=in_specs, out_specs=out_specs, check_vma=False)
```

```python
import jax
import jax.numpy as jnp
import ml_dtypes
import numpy as np
from jax import lax
from jax.experimental import pallas as pl
from jax.experimental.pallas import tpu as pltpu
from jax.sharding import PartitionSpec as P

BLOCK_ROWS = 16
SLOT_CAP = 2
HALF_TAPS = 10
NTAPS = 2 * HALF_TAPS + 1
DEGREE = 6
NPOW = DEGREE + 1
VISITS = 2
BASIS_COUNT = 28
TERMS = 29
GROUPS = 16
TILE = 64
SPAN = 96
SIGMA = 2.0
MARGIN = 16
MIB = 1 << 20


def taps_table():
    places = np.arange(-HALF_TAPS, HALF_TAPS + 1) * 1.0
    basis_rows = []
    for exponent in range(NPOW):
        vector = places**exponent * np.exp(-(places**2) / (2.0 * SIGMA**2))
        for earlier in basis_rows:
            vector = vector - np.dot(earlier, vector) * earlier
        vector = vector / np.sqrt(np.dot(vector, vector))
        basis_rows.append(vector)
    table = np.stack(basis_rows).astype(np.float32)
    return table.astype(ml_dtypes.bfloat16).astype(np.float32)


def band(taps_row, count_out, count_in, shift=0):
    out = np.zeros((count_out, count_in), np.float32)
    for row in range(count_out):
        out[row, row + shift : row + shift + NTAPS] = taps_row
    return out


def column_table(taps):
    return np.concatenate([band(taps[j], 128, 256).T for j in range(NPOW)], axis=1)


def row_bands(taps):
    return np.stack([band(taps[i], TILE, SPAN, MARGIN - HALF_TAPS) for i in range(NPOW)])


def row_table(taps):
    bands = row_bands(taps)
    bands = bands.reshape(NPOW, TILE // 8, 8, SPAN)
    pieces = []
    for j in range(NPOW):
        pieces.append(bands[: NPOW - j].transpose(1, 0, 2, 3).reshape(-1, SPAN))
    return np.concatenate(pieces, axis=0)


def params(mib):
    return pltpu.CompilerParams(vmem_limit_bytes=mib * MIB)


def describe_kernel(dest, offset, visit, bad, meta, row_count):
    count = dest.shape[1]
    slots = meta.shape[0]
    goal = jnp.broadcast_to(dest[...].astype(jnp.float32), (count, count))
    earlier = lax.broadcasted_iota(jnp.int32, (count, count), 0) < lax.broadcasted_iota(jnp.int32, (count, count), 1)
    rank = jnp.sum(jnp.where((jnp.transpose(goal) == goal) & earlier, 1.0, 0.0), axis=0, keepdims=True)
    slot = goal[0:1, :] * SLOT_CAP + rank
    own = lax.broadcasted_iota(jnp.int32, (slots, count), 0).astype(jnp.float32) == slot
    pick = jnp.where(own, 1.0, 0.0)
    start = (visit[...] * row_count + offset[...] + 1).astype(jnp.float32)
    landing = jnp.sum(jnp.where(own, start, 0.0), axis=1, keepdims=True) - 1.0
    words = lax.dot_general(
        pick,
        bad[...].astype(jnp.float32),
        (((1,), (1,)), ((), ())),
        precision=lax.Precision.HIGHEST,
        preferred_element_type=jnp.float32,
    )
    meta[:, 0:BLOCK_ROWS] = words.astype(jnp.int32)
    meta[:, BLOCK_ROWS : BLOCK_ROWS + 1] = landing.astype(jnp.int32)


def describe(dest, offset, visit_id, flags, slots, row_count):
    vmem = pl.BlockSpec(memory_space=pltpu.VMEM)

    def kernel(*refs):
        describe_kernel(*refs, row_count=row_count)

    return pl.pallas_call(
        kernel,
        out_shape=jax.ShapeDtypeStruct((slots, 1 + BLOCK_ROWS), jnp.int32),
        in_specs=[vmem] * 4,
        out_specs=vmem,
        name="describe_blocks",
    )(dest[None, :], offset[None, :], visit_id[None, :], flags)


def pack_kernel(dest_hbm, bad_hbm, blocks, send, dest, bad, buf, out, zero, spread, cnt, where, sem_small, sem_in, sem_out):
    count = blocks.shape[0]
    cols = blocks.shape[2]
    slots = send.shape[0]
    group = min(8, count)
    small = [
        pltpu.make_async_copy(dest_hbm, dest, sem_small.at[0]),
        pltpu.make_async_copy(bad_hbm, bad, sem_small.at[1]),
    ]
    for item in small:
        item.start()
    for k in range(count // group):
        part = pl.ds(k * group, group)
        pltpu.make_async_copy(blocks.at[part], buf.at[part], sem_in.at[k]).start()

    def reset(d, carry):
        cnt[d] = 0
        return carry

    def locate(n, carry):
        d = dest[n]
        rank = cnt[d]
        cnt[d] = rank + 1
        where[n] = d * SLOT_CAP + rank
        return carry

    def blank(d, carry):
        for r in range(SLOT_CAP):

            @pl.when(cnt[d] <= r)
            def _():
                pltpu.make_async_copy(zero, send.at[d * SLOT_CAP + r], sem_out).start()

        return carry

    zero[...] = jnp.zeros_like(zero)
    lax.fori_loop(0, slots // SLOT_CAP, reset, 0, unroll=8)
    for item in small:
        item.wait()
    lax.fori_loop(0, count, locate, 0, unroll=4)
    lax.fori_loop(0, slots // SLOT_CAP, blank, 0, unroll=4)
    row_id = lax.broadcasted_iota(jnp.int32, (128, 128), 0)
    for q in range(cols // 128):
        spread[:, q * 128 : (q + 1) * 128] = jnp.where(row_id == q * GROUPS // (cols // 128), 1.0, 0.0).astype(jnp.bfloat16)
    flags = bad[...]
    lane = lax.broadcasted_iota(jnp.int32, (BLOCK_ROWS, 128), 1)
    shift = jnp.minimum(lane, GROUPS)
    for k in range(count // group):
        rows = []
        for n in range(k * group, (k + 1) * group):
            word = jnp.broadcast_to(flags[:, n : n + 1], (BLOCK_ROWS, 128))
            bit = jnp.bitwise_and(jnp.right_shift(word, shift), 1)
            rows.append((1 - bit).astype(jnp.float32))
        good = jnp.concatenate(rows, axis=0).astype(jnp.bfloat16)
        mask = jnp.dot(good, spread[...], preferred_element_type=jnp.float32).astype(jnp.bfloat16)
        part = pl.ds(k * group, group)
        pltpu.make_async_copy(blocks.at[part], buf.at[part], sem_in.at[k]).wait()
        out[part] = buf[part] * mask.reshape(group, BLOCK_ROWS, cols)
        for n in range(k * group, (k + 1) * group):
            pltpu.make_async_copy(out.at[n], send.at[where[n]], sem_out).start()
    pltpu.make_async_copy(send, send, sem_out).wait()


def pack(dest, flags, blocks, slots):
    count, _, cols = blocks.shape
    hbm = pl.BlockSpec(memory_space=pltpu.HBM)
    return pl.pallas_call(
        pack_kernel,
        out_shape=pltpu.HBM((slots, BLOCK_ROWS, cols), jnp.bfloat16),
        in_specs=[hbm, hbm, hbm],
        out_specs=hbm,
        scratch_shapes=[
            pltpu.SMEM((count,), jnp.int32),
            pltpu.VMEM((BLOCK_ROWS, count), jnp.int32),
            pltpu.VMEM((count, BLOCK_ROWS, cols), jnp.bfloat16),
            pltpu.VMEM((count, BLOCK_ROWS, cols), jnp.bfloat16),
            pltpu.VMEM((BLOCK_ROWS, cols), jnp.bfloat16),
            pltpu.VMEM((128, cols), jnp.bfloat16),
            pltpu.SMEM((slots // SLOT_CAP,), jnp.int32),
            pltpu.SMEM((count,), jnp.int32),
            pltpu.SemaphoreType.DMA((2,)),
            pltpu.SemaphoreType.DMA((max(1, count // 8),)),
            pltpu.SemaphoreType.DMA,
        ],
        compiler_params=params(24),
        name="pack_blocks",
    )(*(pltpu.with_memory_space_constraint(item, pltpu.HBM) for item in (dest, flags, blocks)))


def cover_kernel(meta, placing, spread):
    slots = meta.shape[0]
    cols = spread.shape[1]
    lines = placing.shape[1]
    rows = placing.shape[0]
    words = jnp.transpose(meta[...].astype(jnp.float32))
    slot_id = lax.broadcasted_iota(jnp.int32, (slots, lines), 0)
    line_id = lax.broadcasted_iota(jnp.int32, (slots, lines), 1)
    pick = jnp.where(slot_id == line_id // BLOCK_ROWS, 1.0, 0.0).astype(jnp.float32)
    wide = jnp.dot(words, pick, precision=lax.Precision.HIGHEST, preferred_element_type=jnp.float32)
    lane = lax.broadcasted_iota(jnp.int32, (1, lines), 1)
    inner = lane % BLOCK_ROWS
    start = wide[BLOCK_ROWS : BLOCK_ROWS + 1, :].astype(jnp.int32)
    target = jnp.where(start >= 0, start + inner, -1)
    own = lax.broadcasted_iota(jnp.int32, (BLOCK_ROWS, lines), 0) == inner
    word = jnp.sum(jnp.where(own, wide[0:BLOCK_ROWS, :], 0.0), axis=0, keepdims=True).astype(jnp.int32)
    group = lax.broadcasted_iota(jnp.int32, (128, lines), 0)
    bit = jnp.bitwise_and(jnp.right_shift(jnp.broadcast_to(word, (128, lines)), jnp.minimum(group, GROUPS)), 1)
    good = (1 - bit).astype(jnp.float32).astype(jnp.bfloat16)
    step = 128
    for k in range(rows // step):
        row = lax.broadcasted_iota(jnp.int32, (step, lines), 0) + k * step
        placing[k * step : (k + 1) * step, :] = jnp.where(row == target, 1.0, 0.0).astype(jnp.bfloat16)
    counted = lax.dot_general(placing[...], good, (((1,), (1,)), ((), ())), preferred_element_type=jnp.float32)
    wide_group = cols // GROUPS
    for q in range(GROUPS):
        spread[:, q * wide_group : (q + 1) * wide_group] = jnp.broadcast_to(
            counted[:, q : q + 1], (rows, wide_group)
        ).astype(jnp.bfloat16)


def cover(got_meta, row_count, cols):
    slots = got_meta.shape[0]
    vmem = pl.BlockSpec(memory_space=pltpu.VMEM)
    return pl.pallas_call(
        cover_kernel,
        out_shape=(
            jax.ShapeDtypeStruct((VISITS * row_count, slots * BLOCK_ROWS), jnp.bfloat16),
            jax.ShapeDtypeStruct((VISITS * row_count, cols), jnp.bfloat16),
        ),
        in_specs=[vmem],
        out_specs=(vmem, vmem),
        compiler_params=params(24),
        name="coverage",
    )(got_meta)


def column_kernel(padded, table, out):
    for k in range(out.shape[2] // 128):
        window = padded[:, k * 128 : k * 128 + 256]
        result = jnp.dot(window, table[...], preferred_element_type=jnp.float32)
        for j in range(NPOW):
            out[j, :, k * 128 : (k + 1) * 128] = result[:, j * 128 : (j + 1) * 128].astype(jnp.bfloat16)


def column_pass(padded, taps, cols):
    rows = padded.shape[0]
    vmem = pl.BlockSpec(memory_space=pltpu.VMEM)
    table = jnp.asarray(column_table(taps).astype(ml_dtypes.bfloat16))
    return pl.pallas_call(
        column_kernel,
        out_shape=jax.ShapeDtypeStruct((NPOW, rows, cols), jnp.bfloat16),
        in_specs=[vmem, vmem],
        out_specs=vmem,
        compiler_params=params(24),
        name="column_pass",
    )(padded, table)


GRAM_ROWS = 240


def gram_kernel(images, table, count, out, stage, acc):
    cols = images.shape[2]
    rows = count.shape[0] // VISITS
    chunk = stage.shape[1]
    ones = jnp.ones((8, chunk), jnp.float32)
    blank = jnp.zeros((8, chunk), jnp.float32)
    acc[...] = jnp.zeros_like(acc)

    def tile(step, carry):
        first = pl.multiple_of(step * TILE, TILE)
        for k in range(cols // chunk):
            lanes = slice(k * chunk, (k + 1) * chunk)
            at = 0
            for j in range(NPOW):
                size = TILE * (NPOW - j)
                window = images[j, pl.ds(first, SPAN), lanes]
                stage[at : at + size, :] = jnp.dot(
                    table[at : at + size, :], window, preferred_element_type=jnp.float32
                )
                at += size
            for pair in range(TILE // 16):
                seen = [
                    jnp.minimum(
                        count[pl.ds(pl.multiple_of(v * rows + first + pair * 16, 16), 16), lanes].astype(jnp.float32), 1.0
                    )
                    for v in range(VISITS)
                ]
                for half in range(2):
                    cb = pair * 2 + half
                    pieces = []
                    at = 0
                    for j in range(NPOW):
                        size = 8 * (NPOW - j)
                        pieces.append(stage[at + cb * size : at + (cb + 1) * size, :])
                        at += TILE * (NPOW - j)
                    basis = jnp.concatenate(pieces + [ones, blank], axis=0)
                    scaled = []
                    for v in range(VISITS):
                        w = seen[v][half * 8 : half * 8 + 8]
                        scaled.append(
                            (basis.reshape(GRAM_ROWS // 8, 8, chunk) * w[None])
                            .reshape(GRAM_ROWS, chunk)
                            .astype(jnp.bfloat16)
                        )
                    acc[...] += lax.dot_general(
                        jnp.concatenate(scaled, axis=0),
                        basis.astype(jnp.bfloat16),
                        (((1,), (1,)), ((), ())),
                        preferred_element_type=jnp.float32,
                    )
        return carry

    lax.fori_loop(0, rows // TILE, tile, 0)
    row_id = lax.broadcasted_iota(jnp.int32, (GRAM_ROWS, GRAM_ROWS), 0)
    lane_id = lax.broadcasted_iota(jnp.int32, (GRAM_ROWS, GRAM_ROWS), 1)
    same = (row_id % 8) == (lane_id % 8)
    gather = jnp.where(
        lax.broadcasted_iota(jnp.int32, (GRAM_ROWS, 128), 0) // 8
        == lax.broadcasted_iota(jnp.int32, (GRAM_ROWS, 128), 1),
        1.0,
        0.0,
    )
    for v in range(VISITS):
        kept = jnp.where(same, acc[v * GRAM_ROWS : (v + 1) * GRAM_ROWS, :], 0.0)
        kept = jnp.sum(kept.reshape(GRAM_ROWS // 8, 8, GRAM_ROWS), axis=1)
        full = jnp.dot(kept, gather, precision=lax.Precision.HIGHEST, preferred_element_type=jnp.float32)
        out[v] = full[:TERMS, :TERMS]


def gram(images, count, taps):
    vmem = pl.BlockSpec(memory_space=pltpu.VMEM)
    table = jnp.asarray(row_table(taps).astype(ml_dtypes.bfloat16))
    return pl.pallas_call(
        gram_kernel,
        out_shape=jax.ShapeDtypeStruct((VISITS, TERMS, TERMS), jnp.float32),
        in_specs=[vmem, vmem, vmem],
        out_specs=vmem,
        scratch_shapes=[
            pltpu.VMEM((BASIS_COUNT * TILE, 1024), jnp.float32),
            pltpu.VMEM((VISITS * GRAM_ROWS, GRAM_ROWS), jnp.float32),
        ],
        compiler_params=params(28),
        name="normal_matrix",
    )(images, table, count)


def place_kernel(got, placing, count, source, table, science, sums, images, buf, acc, sem_got, sem_img):
    rows = science.shape[1]
    cols = science.shape[2]
    chunk = 256
    copies = []
    for c in range(cols // chunk):
        lanes = slice(c * chunk, (c + 1) * chunk)
        copies.append(
            (
                pltpu.make_async_copy(got.at[:, :, lanes], buf.at[:, :, lanes], sem_got.at[c]),
                pltpu.make_async_copy(source.at[:, :, lanes], images.at[:, :, lanes], sem_img.at[c]),
            )
        )
        for item in copies[-1]:
            item.start()
    partial = None
    total = [jnp.zeros((8, 128), jnp.float32) for _ in range(VISITS)]
    for c in range(cols // chunk):
        lanes = slice(c * chunk, (c + 1) * chunk)
        copies[c][0].wait()
        summed = jnp.dot(placing[...], buf[:, :, lanes].reshape(-1, chunk), preferred_element_type=jnp.float32)
        spread = count[:, lanes].astype(jnp.float32)
        value = (summed / jnp.maximum(spread, 1.0)).astype(jnp.bfloat16)
        weighted = value * jnp.minimum(spread, 1.0).astype(jnp.bfloat16)
        for v in range(VISITS):
            science[v, :, lanes] = value[v * rows : (v + 1) * rows, :]
            part = weighted[v * rows : (v + 1) * rows, :].astype(jnp.float32)
            fold = jnp.sum(part.reshape(rows // 8, 8, chunk), axis=0)
            for k in range(chunk // 128):
                total[v] = total[v] + fold[:, k * 128 : (k + 1) * 128]
        copies[c][1].wait()
        for t in range(rows // TILE):
            left = jnp.concatenate(
                [weighted[v * rows + t * TILE : v * rows + (t + 1) * TILE, :] for v in range(VISITS)], axis=0
            )
            right = images[:, t * TILE : t * TILE + SPAN, lanes].reshape(NPOW * SPAN, chunk)
            product = lax.dot_general(left, right, (((1,), (1,)), ((), ())), preferred_element_type=jnp.float32)
            partial = product if partial is None else partial + product
    acc[...] = partial
    row_id = lax.broadcasted_iota(jnp.int32, (32, 128), 0)
    lane_id = lax.broadcasted_iota(jnp.int32, (32, 128), 1)
    result = jnp.zeros((32, 128), jnp.float32)
    for v in range(VISITS):
        parts = []
        for j in range(NPOW):
            cross = acc[v * TILE : (v + 1) * TILE, j * SPAN : (j + 1) * SPAN]
            for i in range(NPOW - j):
                parts.append(jnp.sum(cross * table[i], axis=0, keepdims=True))
        parts.append(jnp.zeros((32 - BASIS_COUNT, SPAN), jnp.float32))
        item = jnp.sum(jnp.concatenate(parts, axis=0), axis=1, keepdims=True)
        flat = jnp.sum(jnp.sum(total[v], axis=0, keepdims=True), axis=1, keepdims=True)
        item = jnp.where(row_id == BASIS_COUNT, flat, item)
        result = result + jnp.where(lane_id == v, item, 0.0)
    sums[...] = result


def place(got, placing, count, images, bands, row_count):
    slots, _, cols = got.shape
    chunks = cols // 256
    table = jnp.asarray(bands)
    vmem = pl.BlockSpec(memory_space=pltpu.VMEM)
    hbm = pl.BlockSpec(memory_space=pltpu.HBM)
    return pl.pallas_call(
        place_kernel,
        out_shape=(
            jax.ShapeDtypeStruct((VISITS, row_count, cols), jnp.bfloat16),
            jax.ShapeDtypeStruct((32, 128), jnp.float32),
            jax.ShapeDtypeStruct(images.shape, jnp.bfloat16),
        ),
        in_specs=[hbm, vmem, vmem, hbm, vmem],
        out_specs=(vmem, vmem, vmem),
        scratch_shapes=[
            pltpu.VMEM(got.shape, jnp.bfloat16),
            pltpu.VMEM((VISITS * TILE, NPOW * SPAN), jnp.float32),
            pltpu.SemaphoreType.DMA((chunks,)),
            pltpu.SemaphoreType.DMA((chunks,)),
        ],
        compiler_params=params(40),
        name="place_and_correlate",
    )(
        pltpu.with_memory_space_constraint(got, pltpu.HBM),
        placing,
        count,
        pltpu.with_memory_space_constraint(images, pltpu.HBM),
        table,
    )


def model_kernel(sums, inverse, table, images, science, count, out, coeffs, wide, narrow, buf, sem):
    rows = science.shape[1]
    cols = science.shape[2]
    chunk = 256
    rhs = sums[0:32, :]
    for k in range(1, sums.shape[0] // 32):
        rhs = rhs + sums[k * 32 : (k + 1) * 32, :]
    level = []
    for v in range(VISITS):
        row = jnp.sum(inverse[v] * rhs[:, v : v + 1], axis=0, keepdims=True)
        coeffs[v : v + 1, :] = row[:, :TERMS]
        level.append(row[:, BASIS_COUNT : BASIS_COUNT + 1])
        index = 0
        for j in range(NPOW):
            kernel = jnp.zeros((TILE, SPAN), jnp.float32)
            for i in range(NPOW - j):
                kernel = kernel + row[:, index : index + 1] * table[i]
                index += 1
            wide[v * TILE : (v + 1) * TILE, j * SPAN : (j + 1) * SPAN] = kernel
    narrow[...] = wide[...].astype(jnp.bfloat16)
    copies = []
    for c in range(cols // chunk):
        lanes = slice(c * chunk, (c + 1) * chunk)
        for t in range(rows // TILE):
            right = images[:, t * TILE : t * TILE + SPAN, lanes].reshape(NPOW * SPAN, chunk)
            model = jnp.dot(narrow[...], right, preferred_element_type=jnp.float32)
            for v in range(VISITS):
                at = slice(t * TILE, (t + 1) * TILE)
                full = model[v * TILE : (v + 1) * TILE, :] + level[v]
                seen = count[v * rows + t * TILE : v * rows + (t + 1) * TILE, lanes]
                weight = jnp.minimum(seen.astype(jnp.float32), 1.0)
                buf[v, at, lanes] = (weight * (science[v, at, lanes].astype(jnp.float32) - full)).astype(jnp.bfloat16)
        copies.append(pltpu.make_async_copy(buf.at[:, :, lanes], out.at[:, :, lanes], sem.at[c]))
        copies[-1].start()
    for item in copies:
        item.wait()


def model(sums, inverse, images, science, count, bands):
    _, rows, cols = science.shape
    table = jnp.asarray(bands)
    vmem = pl.BlockSpec(memory_space=pltpu.VMEM)
    return pl.pallas_call(
        model_kernel,
        out_shape=(
            pltpu.HBM((VISITS, rows, cols), jnp.bfloat16),
            jax.ShapeDtypeStruct((VISITS, TERMS), jnp.float32),
        ),
        in_specs=[vmem] * 6,
        out_specs=(pl.BlockSpec(memory_space=pltpu.HBM), vmem),
        scratch_shapes=[
            pltpu.VMEM((VISITS * TILE, NPOW * SPAN), jnp.float32),
            pltpu.VMEM((VISITS * TILE, NPOW * SPAN), jnp.bfloat16),
            pltpu.VMEM((VISITS, rows, cols), jnp.bfloat16),
            pltpu.SemaphoreType.DMA((cols // 256,)),
        ],
        compiler_params=params(28),
        name="model_and_difference",
    )(sums, inverse, table, images, science, count)


def inverse_of(matrix):
    eye = jnp.broadcast_to(jnp.eye(TERMS, dtype=jnp.float32), matrix.shape)
    lower = jnp.linalg.cholesky(matrix)
    half = jax.scipy.linalg.solve_triangular(lower, eye, lower=True)
    return jnp.einsum("vkb,vkc->vbc", half, half, precision=lax.Precision.HIGHEST)


def halo(rows):
    count = lax.axis_size("visit")
    up = [(i, i + 1) for i in range(count - 1)]
    down = [(i + 1, i) for i in range(count - 1)]
    above = lax.ppermute(rows[-MARGIN:], "visit", up)
    below = lax.ppermute(rows[:MARGIN], "visit", down)
    return above, below


def body(template, blocks, dest, offset, visit_id, badmask):
    row_count = template.shape[1]
    cols = template.shape[2]
    axes = ("patch", "visit")
    sources = lax.axis_size("patch") * lax.axis_size("visit")
    slots = sources * SLOT_CAP
    taps = taps_table()
    bands = row_bands(taps)

    flags = badmask.T
    meta = describe(dest, offset, visit_id, flags, slots, row_count)
    got_meta = lax.all_to_all(meta, axes, split_axis=0, concat_axis=0, tiled=True)
    send = pack(dest, flags, blocks, slots)
    send, got_meta, rows = lax.optimization_barrier((send, got_meta, template[0]))
    got = lax.all_to_all(send, axes, split_axis=0, concat_axis=0, tiled=True)

    above, below = halo(rows)
    tall = jnp.concatenate([above, rows, below], axis=0)
    padded = jnp.pad(tall, ((0, 0), (HALF_TAPS, 128 - HALF_TAPS)))
    images = column_pass(padded, taps, cols)
    placing, count = cover(got_meta, row_count, cols)

    normal = lax.psum(gram(images, count, taps), "visit")
    inverse = jnp.pad(inverse_of(normal), ((0, 0), (0, 32 - TERMS), (0, 128 - TERMS)))

    science, sums, images = place(got, placing, count, images, bands, row_count)
    sums = lax.all_gather(sums, "visit", axis=0, tiled=True)
    difference, coeffs = model(sums, inverse, images, science, count, bands)
    return (difference[:, None], coeffs[:, None])


def solution(mesh):
    in_specs = (
        P("patch", "visit", None),
        P(("patch", "visit"), None, None),
        P(("patch", "visit")),
        P(("patch", "visit")),
        P(("patch", "visit")),
        P(("patch", "visit"), None),
    )
    out_specs = (P(None, "patch", "visit", None), P(None, "patch", None))
    return jax.shard_map(body, mesh=mesh, in_specs=in_specs, out_specs=out_specs, check_vma=False)
```

```python
import jax
import jax.numpy as jnp
import ml_dtypes
import numpy as np
from jax import lax
from jax.experimental import pallas as pl
from jax.experimental.pallas import tpu as pltpu
from jax.sharding import PartitionSpec as P

BLOCK_ROWS = 16
SLOT_CAP = 2
HALF_TAPS = 10
NTAPS = 2 * HALF_TAPS + 1
DEGREE = 6
NPOW = DEGREE + 1
VISITS = 2
BASIS_COUNT = 28
TERMS = 29
GROUPS = 16
TILE = 64
SPAN = 96
SIGMA = 2.0
MARGIN = 16
MIB = 1 << 20


def taps_table():
    places = np.arange(-HALF_TAPS, HALF_TAPS + 1) * 1.0
    basis_rows = []
    for exponent in range(NPOW):
        vector = places**exponent * np.exp(-(places**2) / (2.0 * SIGMA**2))
        for earlier in basis_rows:
            vector = vector - np.dot(earlier, vector) * earlier
        vector = vector / np.sqrt(np.dot(vector, vector))
        basis_rows.append(vector)
    table = np.stack(basis_rows).astype(np.float32)
    return table.astype(ml_dtypes.bfloat16).astype(np.float32)


def band(taps_row, count_out, count_in, shift=0):
    out = np.zeros((count_out, count_in), np.float32)
    for row in range(count_out):
        out[row, row + shift : row + shift + NTAPS] = taps_row
    return out


def column_table(taps):
    return np.concatenate([band(taps[j], 128, 256).T for j in range(NPOW)], axis=1)


def row_bands(taps):
    return np.stack([band(taps[i], TILE, SPAN, MARGIN - HALF_TAPS) for i in range(NPOW)])


def row_table(taps):
    bands = row_bands(taps)
    bands = bands.reshape(NPOW, TILE // 8, 8, SPAN)
    pieces = []
    for j in range(NPOW):
        pieces.append(bands[: NPOW - j].transpose(1, 0, 2, 3).reshape(-1, SPAN))
    return np.concatenate(pieces, axis=0)


def params(mib):
    return pltpu.CompilerParams(vmem_limit_bytes=mib * MIB)


def describe_kernel(dest, offset, visit, bad, meta, row_count):
    count = dest.shape[1]
    slots = meta.shape[0]
    goal = jnp.broadcast_to(dest[...].astype(jnp.float32), (count, count))
    earlier = lax.broadcasted_iota(jnp.int32, (count, count), 0) < lax.broadcasted_iota(jnp.int32, (count, count), 1)
    rank = jnp.sum(jnp.where((jnp.transpose(goal) == goal) & earlier, 1.0, 0.0), axis=0, keepdims=True)
    slot = goal[0:1, :] * SLOT_CAP + rank
    own = lax.broadcasted_iota(jnp.int32, (slots, count), 0).astype(jnp.float32) == slot
    pick = jnp.where(own, 1.0, 0.0)
    start = (visit[...] * row_count + offset[...] + 1).astype(jnp.float32)
    landing = jnp.sum(jnp.where(own, start, 0.0), axis=1, keepdims=True) - 1.0
    words = lax.dot_general(
        pick,
        bad[...].astype(jnp.float32),
        (((1,), (1,)), ((), ())),
        precision=lax.Precision.HIGHEST,
        preferred_element_type=jnp.float32,
    )
    meta[:, 0:BLOCK_ROWS] = words.astype(jnp.int32)
    meta[:, BLOCK_ROWS : BLOCK_ROWS + 1] = landing.astype(jnp.int32)


def describe(dest, offset, visit_id, flags, slots, row_count):
    vmem = pl.BlockSpec(memory_space=pltpu.VMEM)

    def kernel(*refs):
        describe_kernel(*refs, row_count=row_count)

    return pl.pallas_call(
        kernel,
        out_shape=jax.ShapeDtypeStruct((slots, 1 + BLOCK_ROWS), jnp.int32),
        in_specs=[vmem] * 4,
        out_specs=vmem,
        name="describe_blocks",
    )(dest[None, :], offset[None, :], visit_id[None, :], flags)


def pack_kernel(dest_hbm, bad_hbm, blocks, send, dest, bad, buf, out, zero, spread, cnt, where, sem_small, sem_in, sem_out):
    count = blocks.shape[0]
    cols = blocks.shape[2]
    slots = send.shape[0]
    group = min(8, count)
    small = [
        pltpu.make_async_copy(dest_hbm, dest, sem_small.at[0]),
        pltpu.make_async_copy(bad_hbm, bad, sem_small.at[1]),
    ]
    for item in small:
        item.start()
    for k in range(count // group):
        part = pl.ds(k * group, group)
        pltpu.make_async_copy(blocks.at[part], buf.at[part], sem_in.at[k]).start()

    def reset(d, carry):
        cnt[d] = 0
        return carry

    def locate(n, carry):
        d = dest[n]
        rank = cnt[d]
        cnt[d] = rank + 1
        where[n] = d * SLOT_CAP + rank
        return carry

    def blank(d, carry):
        for r in range(SLOT_CAP):

            @pl.when(cnt[d] <= r)
            def _():
                pltpu.make_async_copy(zero, send.at[d * SLOT_CAP + r], sem_out).start()

        return carry

    zero[...] = jnp.zeros_like(zero)
    lax.fori_loop(0, slots // SLOT_CAP, reset, 0, unroll=8)
    for item in small:
        item.wait()
    lax.fori_loop(0, count, locate, 0, unroll=4)
    lax.fori_loop(0, slots // SLOT_CAP, blank, 0, unroll=4)
    row_id = lax.broadcasted_iota(jnp.int32, (128, 128), 0)
    for q in range(cols // 128):
        spread[:, q * 128 : (q + 1) * 128] = jnp.where(row_id == q * GROUPS // (cols // 128), 1.0, 0.0).astype(jnp.bfloat16)
    flags = bad[...]
    lane = lax.broadcasted_iota(jnp.int32, (BLOCK_ROWS, 128), 1)
    shift = jnp.minimum(lane, GROUPS)
    for k in range(count // group):
        rows = []
        for n in range(k * group, (k + 1) * group):
            word = jnp.broadcast_to(flags[:, n : n + 1], (BLOCK_ROWS, 128))
            bit = jnp.bitwise_and(jnp.right_shift(word, shift), 1)
            rows.append((1 - bit).astype(jnp.float32))
        good = jnp.concatenate(rows, axis=0).astype(jnp.bfloat16)
        mask = jnp.dot(good, spread[...], preferred_element_type=jnp.float32).astype(jnp.bfloat16)
        part = pl.ds(k * group, group)
        pltpu.make_async_copy(blocks.at[part], buf.at[part], sem_in.at[k]).wait()
        out[part] = buf[part] * mask.reshape(group, BLOCK_ROWS, cols)
        for n in range(k * group, (k + 1) * group):
            pltpu.make_async_copy(out.at[n], send.at[where[n]], sem_out).start()
    pltpu.make_async_copy(send, send, sem_out).wait()


def pack(dest, flags, blocks, slots):
    count, _, cols = blocks.shape
    hbm = pl.BlockSpec(memory_space=pltpu.HBM)
    return pl.pallas_call(
        pack_kernel,
        out_shape=pltpu.HBM((slots, BLOCK_ROWS, cols), jnp.bfloat16),
        in_specs=[hbm, hbm, hbm],
        out_specs=hbm,
        scratch_shapes=[
            pltpu.SMEM((count,), jnp.int32),
            pltpu.VMEM((BLOCK_ROWS, count), jnp.int32),
            pltpu.VMEM((count, BLOCK_ROWS, cols), jnp.bfloat16),
            pltpu.VMEM((count, BLOCK_ROWS, cols), jnp.bfloat16),
            pltpu.VMEM((BLOCK_ROWS, cols), jnp.bfloat16),
            pltpu.VMEM((128, cols), jnp.bfloat16),
            pltpu.SMEM((slots // SLOT_CAP,), jnp.int32),
            pltpu.SMEM((count,), jnp.int32),
            pltpu.SemaphoreType.DMA((2,)),
            pltpu.SemaphoreType.DMA((max(1, count // 8),)),
            pltpu.SemaphoreType.DMA,
        ],
        compiler_params=params(24),
        name="pack_blocks",
    )(*(pltpu.with_memory_space_constraint(item, pltpu.HBM) for item in (dest, flags, blocks)))


def cover_kernel(meta, placing, spread, factor):
    slots = meta.shape[0]
    cols = spread.shape[1]
    lines = placing.shape[1]
    rows = placing.shape[0]
    words = jnp.transpose(meta[...].astype(jnp.float32))
    slot_id = lax.broadcasted_iota(jnp.int32, (slots, lines), 0)
    line_id = lax.broadcasted_iota(jnp.int32, (slots, lines), 1)
    pick = jnp.where(slot_id == line_id // BLOCK_ROWS, 1.0, 0.0).astype(jnp.float32)
    wide = jnp.dot(words, pick, precision=lax.Precision.HIGHEST, preferred_element_type=jnp.float32)
    lane = lax.broadcasted_iota(jnp.int32, (1, lines), 1)
    inner = lane % BLOCK_ROWS
    start = wide[BLOCK_ROWS : BLOCK_ROWS + 1, :].astype(jnp.int32)
    target = jnp.where(start >= 0, start + inner, -1)
    own = lax.broadcasted_iota(jnp.int32, (BLOCK_ROWS, lines), 0) == inner
    word = jnp.sum(jnp.where(own, wide[0:BLOCK_ROWS, :], 0.0), axis=0, keepdims=True).astype(jnp.int32)
    group = lax.broadcasted_iota(jnp.int32, (128, lines), 0)
    bit = jnp.bitwise_and(jnp.right_shift(jnp.broadcast_to(word, (128, lines)), jnp.minimum(group, GROUPS)), 1)
    good = (1 - bit).astype(jnp.float32).astype(jnp.bfloat16)
    step = 128
    for k in range(rows // step):
        row = lax.broadcasted_iota(jnp.int32, (step, lines), 0) + k * step
        placing[k * step : (k + 1) * step, :] = jnp.where(row == target, 1.0, 0.0).astype(jnp.bfloat16)
    counted = lax.dot_general(placing[...], good, (((1,), (1,)), ((), ())), preferred_element_type=jnp.float32)
    factor[...] = jnp.minimum(counted, 1.0) / jnp.maximum(counted, 1.0)
    wide_group = cols // GROUPS
    for q in range(GROUPS):
        spread[:, q * wide_group : (q + 1) * wide_group] = jnp.broadcast_to(
            counted[:, q : q + 1], (rows, wide_group)
        ).astype(jnp.bfloat16)


def cover(got_meta, row_count, cols):
    slots = got_meta.shape[0]
    vmem = pl.BlockSpec(memory_space=pltpu.VMEM)
    return pl.pallas_call(
        cover_kernel,
        out_shape=(
            jax.ShapeDtypeStruct((VISITS * row_count, slots * BLOCK_ROWS), jnp.bfloat16),
            jax.ShapeDtypeStruct((VISITS * row_count, cols), jnp.bfloat16),
            jax.ShapeDtypeStruct((VISITS * row_count, 128), jnp.float32),
        ),
        in_specs=[vmem],
        out_specs=(vmem, vmem, vmem),
        compiler_params=params(24),
        name="coverage",
    )(got_meta)


def column_kernel(padded, table, out):
    for k in range(out.shape[2] // 128):
        window = padded[:, k * 128 : k * 128 + 256]
        result = jnp.dot(window, table[...], preferred_element_type=jnp.float32)
        for j in range(NPOW):
            out[j, :, k * 128 : (k + 1) * 128] = result[:, j * 128 : (j + 1) * 128].astype(jnp.bfloat16)


def column_pass(padded, taps, cols):
    rows = padded.shape[0]
    vmem = pl.BlockSpec(memory_space=pltpu.VMEM)
    table = jnp.asarray(column_table(taps).astype(ml_dtypes.bfloat16))
    return pl.pallas_call(
        column_kernel,
        out_shape=jax.ShapeDtypeStruct((NPOW, rows, cols), jnp.bfloat16),
        in_specs=[vmem, vmem],
        out_specs=vmem,
        compiler_params=params(24),
        name="column_pass",
    )(padded, table)


GRAM_ROWS = 240


def gram_kernel(images, table, count, out, stage, acc):
    cols = images.shape[2]
    rows = count.shape[0] // VISITS
    chunk = stage.shape[1]
    ones = jnp.ones((8, chunk), jnp.float32)
    blank = jnp.zeros((8, chunk), jnp.float32)
    acc[...] = jnp.zeros_like(acc)

    def tile(step, carry):
        first = pl.multiple_of(step * TILE, TILE)
        for k in range(cols // chunk):
            lanes = slice(k * chunk, (k + 1) * chunk)
            at = 0
            for j in range(NPOW):
                size = TILE * (NPOW - j)
                window = images[j, pl.ds(first, SPAN), lanes]
                stage[at : at + size, :] = jnp.dot(
                    table[at : at + size, :], window, preferred_element_type=jnp.float32
                )
                at += size
            for pair in range(TILE // 16):
                seen = [
                    jnp.minimum(
                        count[pl.ds(pl.multiple_of(v * rows + first + pair * 16, 16), 16), lanes].astype(jnp.float32), 1.0
                    )
                    for v in range(VISITS)
                ]
                for half in range(2):
                    cb = pair * 2 + half
                    pieces = []
                    at = 0
                    for j in range(NPOW):
                        size = 8 * (NPOW - j)
                        pieces.append(stage[at + cb * size : at + (cb + 1) * size, :])
                        at += TILE * (NPOW - j)
                    basis = jnp.concatenate(pieces + [ones, blank], axis=0)
                    scaled = []
                    for v in range(VISITS):
                        w = seen[v][half * 8 : half * 8 + 8]
                        scaled.append(
                            (basis.reshape(GRAM_ROWS // 8, 8, chunk) * w[None])
                            .reshape(GRAM_ROWS, chunk)
                            .astype(jnp.bfloat16)
                        )
                    acc[...] += lax.dot_general(
                        jnp.concatenate(scaled, axis=0),
                        basis.astype(jnp.bfloat16),
                        (((1,), (1,)), ((), ())),
                        preferred_element_type=jnp.float32,
                    )
        return carry

    lax.fori_loop(0, rows // TILE, tile, 0)
    row_id = lax.broadcasted_iota(jnp.int32, (GRAM_ROWS, GRAM_ROWS), 0)
    lane_id = lax.broadcasted_iota(jnp.int32, (GRAM_ROWS, GRAM_ROWS), 1)
    same = (row_id % 8) == (lane_id % 8)
    gather = jnp.where(
        lax.broadcasted_iota(jnp.int32, (GRAM_ROWS, 128), 0) // 8
        == lax.broadcasted_iota(jnp.int32, (GRAM_ROWS, 128), 1),
        1.0,
        0.0,
    )
    for v in range(VISITS):
        kept = jnp.where(same, acc[v * GRAM_ROWS : (v + 1) * GRAM_ROWS, :], 0.0)
        kept = jnp.sum(kept.reshape(GRAM_ROWS // 8, 8, GRAM_ROWS), axis=1)
        full = jnp.dot(kept, gather, precision=lax.Precision.HIGHEST, preferred_element_type=jnp.float32)
        out[v] = full[:TERMS, :TERMS]


def gram(images, count, taps):
    vmem = pl.BlockSpec(memory_space=pltpu.VMEM)
    table = jnp.asarray(row_table(taps).astype(ml_dtypes.bfloat16))
    return pl.pallas_call(
        gram_kernel,
        out_shape=jax.ShapeDtypeStruct((VISITS, TERMS, TERMS), jnp.float32),
        in_specs=[vmem, vmem, vmem],
        out_specs=vmem,
        scratch_shapes=[
            pltpu.VMEM((BASIS_COUNT * TILE, 1024), jnp.float32),
            pltpu.VMEM((VISITS * GRAM_ROWS, GRAM_ROWS), jnp.float32),
        ],
        compiler_params=params(28),
        name="normal_matrix",
    )(images, table, count)


ONES_ROWS = 16
PLACE_CHUNK = 512


def place_kernel(got, placing, factor_hbm, source, table, science, sums, images, buf, acc, factor, sem_got, sem_img, sem_small):
    rows = science.shape[1]
    cols = science.shape[2]
    chunk = PLACE_CHUNK
    group = cols // GROUPS
    small = pltpu.make_async_copy(factor_hbm, factor, sem_small)
    small.start()
    copies = []
    for c in range(cols // chunk):
        lanes = slice(c * chunk, (c + 1) * chunk)
        copies.append(
            (
                pltpu.make_async_copy(got.at[:, :, lanes], buf.at[:, :, lanes], sem_got.at[c]),
                pltpu.make_async_copy(source.at[:, :, lanes], images.at[:, :, lanes], sem_img.at[c]),
            )
        )
    for item in copies[0]:
        item.start()
    partial = None
    ones = jnp.ones((ONES_ROWS, chunk), jnp.bfloat16)
    for c in range(cols // chunk):
        lanes = slice(c * chunk, (c + 1) * chunk)
        copies[c][0].wait()
        if c + 1 < len(copies):
            copies[c + 1][0].start()
        summed = jnp.dot(placing[...], buf[:, :, lanes].reshape(-1, chunk), preferred_element_type=jnp.float32)
        if c == 0:
            small.wait()
        spread = jnp.concatenate(
            [
                jnp.broadcast_to(factor[:, q : q + 1], (VISITS * rows, group))
                for q in range(c * chunk // group, (c + 1) * chunk // group)
            ],
            axis=1,
        )
        value = (summed * spread).astype(jnp.bfloat16)
        for v in range(VISITS):
            science[v, :, lanes] = value[v * rows : (v + 1) * rows, :]
        copies[c][1].wait()
        if c + 1 < len(copies):
            copies[c + 1][1].start()
        for t in range(rows // TILE):
            left = jnp.concatenate(
                [value[v * rows + t * TILE : v * rows + (t + 1) * TILE, :] for v in range(VISITS)], axis=0
            )
            right = images[:, t * TILE : t * TILE + SPAN, lanes].reshape(NPOW * SPAN, chunk)
            right = jnp.concatenate([right, ones], axis=0)
            product = lax.dot_general(left, right, (((1,), (1,)), ((), ())), preferred_element_type=jnp.float32)
            partial = product if partial is None else partial + product
    acc[...] = partial
    row_id = lax.broadcasted_iota(jnp.int32, (32, 128), 0)
    lane_id = lax.broadcasted_iota(jnp.int32, (32, 128), 1)
    result = jnp.zeros((32, 128), jnp.float32)
    for v in range(VISITS):
        parts = []
        for j in range(NPOW):
            cross = acc[v * TILE : (v + 1) * TILE, j * SPAN : (j + 1) * SPAN]
            for i in range(NPOW - j):
                parts.append(jnp.sum(cross * table[i], axis=0, keepdims=True))
        parts.append(jnp.zeros((32 - BASIS_COUNT, SPAN), jnp.float32))
        item = jnp.sum(jnp.concatenate(parts, axis=0), axis=1, keepdims=True)
        flat = jnp.sum(acc[v * TILE : (v + 1) * TILE, NPOW * SPAN : NPOW * SPAN + 1], axis=0, keepdims=True)
        item = jnp.where(row_id == BASIS_COUNT, flat, item)
        result = result + jnp.where(lane_id == v, item, 0.0)
    sums[...] = result


def place(got, placing, factor, images, bands, row_count):
    slots, _, cols = got.shape
    table = jnp.asarray(bands)
    vmem = pl.BlockSpec(memory_space=pltpu.VMEM)
    hbm = pl.BlockSpec(memory_space=pltpu.HBM)
    return pl.pallas_call(
        place_kernel,
        out_shape=(
            jax.ShapeDtypeStruct((VISITS, row_count, cols), jnp.bfloat16),
            jax.ShapeDtypeStruct((32, 128), jnp.float32),
            jax.ShapeDtypeStruct(images.shape, jnp.bfloat16),
        ),
        in_specs=[hbm, vmem, hbm, hbm, vmem],
        out_specs=(vmem, vmem, vmem),
        scratch_shapes=[
            pltpu.VMEM(got.shape, jnp.bfloat16),
            pltpu.VMEM((VISITS * TILE, NPOW * SPAN + ONES_ROWS), jnp.float32),
            pltpu.VMEM(factor.shape, jnp.float32),
            pltpu.SemaphoreType.DMA((cols // PLACE_CHUNK,)),
            pltpu.SemaphoreType.DMA((cols // PLACE_CHUNK,)),
            pltpu.SemaphoreType.DMA,
        ],
        compiler_params=params(40),
        name="place_and_correlate",
    )(
        pltpu.with_memory_space_constraint(got, pltpu.HBM),
        placing,
        pltpu.with_memory_space_constraint(factor, pltpu.HBM),
        pltpu.with_memory_space_constraint(images, pltpu.HBM),
        table,
    )


def model_kernel(sums, inverse, table, images, science, count, out, coeffs, wide, narrow, buf, sem):
    rows = science.shape[1]
    cols = science.shape[2]
    chunk = 256
    rhs = sums[0:32, :]
    for k in range(1, sums.shape[0] // 32):
        rhs = rhs + sums[k * 32 : (k + 1) * 32, :]
    level = []
    for v in range(VISITS):
        row = jnp.sum(inverse[v] * rhs[:, v : v + 1], axis=0, keepdims=True)
        coeffs[v : v + 1, :] = row[:, :TERMS]
        level.append(row[:, BASIS_COUNT : BASIS_COUNT + 1])
        index = 0
        for j in range(NPOW):
            kernel = jnp.zeros((TILE, SPAN), jnp.float32)
            for i in range(NPOW - j):
                kernel = kernel + row[:, index : index + 1] * table[i]
                index += 1
            wide[v * TILE : (v + 1) * TILE, j * SPAN : (j + 1) * SPAN] = kernel
    narrow[...] = wide[...].astype(jnp.bfloat16)
    copies = []
    for c in range(cols // chunk):
        lanes = slice(c * chunk, (c + 1) * chunk)
        for t in range(rows // TILE):
            right = images[:, t * TILE : t * TILE + SPAN, lanes].reshape(NPOW * SPAN, chunk)
            model = jnp.dot(narrow[...], right, preferred_element_type=jnp.float32)
            for v in range(VISITS):
                at = slice(t * TILE, (t + 1) * TILE)
                full = model[v * TILE : (v + 1) * TILE, :] + level[v]
                seen = count[v * rows + t * TILE : v * rows + (t + 1) * TILE, lanes]
                weight = jnp.minimum(seen.astype(jnp.float32), 1.0)
                buf[v, at, lanes] = (science[v, at, lanes].astype(jnp.float32) - weight * full).astype(jnp.bfloat16)
        copies.append(pltpu.make_async_copy(buf.at[:, :, lanes], out.at[:, :, lanes], sem.at[c]))
        copies[-1].start()
    for item in copies:
        item.wait()


def model(sums, inverse, images, science, count, bands):
    _, rows, cols = science.shape
    table = jnp.asarray(bands)
    vmem = pl.BlockSpec(memory_space=pltpu.VMEM)
    return pl.pallas_call(
        model_kernel,
        out_shape=(
            pltpu.HBM((VISITS, rows, cols), jnp.bfloat16),
            jax.ShapeDtypeStruct((VISITS, TERMS), jnp.float32),
        ),
        in_specs=[vmem] * 6,
        out_specs=(pl.BlockSpec(memory_space=pltpu.HBM), vmem),
        scratch_shapes=[
            pltpu.VMEM((VISITS * TILE, NPOW * SPAN), jnp.float32),
            pltpu.VMEM((VISITS * TILE, NPOW * SPAN), jnp.bfloat16),
            pltpu.VMEM((VISITS, rows, cols), jnp.bfloat16),
            pltpu.SemaphoreType.DMA((cols // 256,)),
        ],
        compiler_params=params(28),
        name="model_and_difference",
    )(sums, inverse, table, images, science, count)


def inverse_of(matrix):
    eye = jnp.broadcast_to(jnp.eye(TERMS, dtype=jnp.float32), matrix.shape)
    lower = jnp.linalg.cholesky(matrix)
    half = jax.scipy.linalg.solve_triangular(lower, eye, lower=True)
    return jnp.einsum("vkb,vkc->vbc", half, half, precision=lax.Precision.HIGHEST)


def halo(rows):
    count = lax.axis_size("visit")
    up = [(i, i + 1) for i in range(count - 1)]
    down = [(i + 1, i) for i in range(count - 1)]
    above = lax.ppermute(rows[-MARGIN:], "visit", up)
    below = lax.ppermute(rows[:MARGIN], "visit", down)
    return above, below


def body(template, blocks, dest, offset, visit_id, badmask):
    row_count = template.shape[1]
    cols = template.shape[2]
    axes = ("patch", "visit")
    sources = lax.axis_size("patch") * lax.axis_size("visit")
    slots = sources * SLOT_CAP
    taps = taps_table()
    bands = row_bands(taps)

    flags = badmask.T
    meta = describe(dest, offset, visit_id, flags, slots, row_count)
    got_meta = lax.all_to_all(meta, axes, split_axis=0, concat_axis=0, tiled=True)
    send = pack(dest, flags, blocks, slots)
    send, got_meta, rows = lax.optimization_barrier((send, got_meta, template[0]))
    got = lax.all_to_all(send, axes, split_axis=0, concat_axis=0, tiled=True)

    above, below = halo(rows)
    tall = jnp.concatenate([above, rows, below], axis=0)
    padded = jnp.pad(tall, ((0, 0), (HALF_TAPS, 128 - HALF_TAPS)))
    images = column_pass(padded, taps, cols)
    placing, count, factor = cover(got_meta, row_count, cols)

    shares = lax.all_gather(gram(images, count, taps), "visit", axis=0, tiled=False)
    normal = jnp.sum(shares, axis=0)
    inverse = jnp.pad(inverse_of(normal), ((0, 0), (0, 32 - TERMS), (0, 128 - TERMS)))

    science, sums, images = place(got, placing, factor, images, bands, row_count)
    sums = lax.all_gather(sums, "visit", axis=0, tiled=True)
    difference, coeffs = model(sums, inverse, images, science, count, bands)
    return (difference[:, None], coeffs[:, None])


def solution(mesh):
    in_specs = (
        P("patch", "visit", None),
        P(("patch", "visit"), None, None),
        P(("patch", "visit")),
        P(("patch", "visit")),
        P(("patch", "visit")),
        P(("patch", "visit"), None),
    )
    out_specs = (P(None, "patch", "visit", None), P(None, "patch", None))
    return jax.shard_map(body, mesh=mesh, in_specs=in_specs, out_specs=out_specs, check_vma=False)
```

```python
import jax
import jax.numpy as jnp
import ml_dtypes
import numpy as np
from jax import lax
from jax.experimental import pallas as pl
from jax.experimental.pallas import tpu as pltpu
from jax.sharding import PartitionSpec as P

BLOCK_ROWS = 16
SLOT_CAP = 2
HALF_TAPS = 10
NTAPS = 2 * HALF_TAPS + 1
DEGREE = 6
NPOW = DEGREE + 1
VISITS = 2
BASIS_COUNT = 28
TERMS = 29
GROUPS = 16
TILE = 64
SPAN = 96
SIGMA = 2.0
MARGIN = 16
MIB = 1 << 20


def taps_table():
    places = np.arange(-HALF_TAPS, HALF_TAPS + 1) * 1.0
    basis_rows = []
    for exponent in range(NPOW):
        vector = places**exponent * np.exp(-(places**2) / (2.0 * SIGMA**2))
        for earlier in basis_rows:
            vector = vector - np.dot(earlier, vector) * earlier
        vector = vector / np.sqrt(np.dot(vector, vector))
        basis_rows.append(vector)
    table = np.stack(basis_rows).astype(np.float32)
    return table.astype(ml_dtypes.bfloat16).astype(np.float32)


def band(taps_row, count_out, count_in, shift=0):
    out = np.zeros((count_out, count_in), np.float32)
    for row in range(count_out):
        out[row, row + shift : row + shift + NTAPS] = taps_row
    return out


def column_table(taps):
    return np.concatenate([band(taps[j], 128, 256).T for j in range(NPOW)], axis=1)


def row_bands(taps):
    return np.stack([band(taps[i], TILE, SPAN, MARGIN - HALF_TAPS) for i in range(NPOW)])


def row_table(taps):
    bands = row_bands(taps)
    bands = bands.reshape(NPOW, TILE // 8, 8, SPAN)
    pieces = []
    for j in range(NPOW):
        pieces.append(bands[: NPOW - j].transpose(1, 0, 2, 3).reshape(-1, SPAN))
    return np.concatenate(pieces, axis=0)


def params(mib):
    return pltpu.CompilerParams(vmem_limit_bytes=mib * MIB)


FIRST = 4
META_ROWS = 8


def first_kernel(dest_row_hbm, offset_hbm, visit_hbm, flags_hbm, dest_hbm, blocks, send, dest_row, offset, visit, flags, dest, buf, out, zero, wide, narrow, cnt, where, sem_small, sem_in, sem_out, row_count):
    count = blocks.shape[0]
    sources = send.shape[0]
    data_rows = SLOT_CAP * FIRST * BLOCK_ROWS
    slot_rows = FIRST * BLOCK_ROWS
    width = buf.shape[2]
    small = [
        pltpu.make_async_copy(source, target, sem_small.at[k])
        for k, (source, target) in enumerate(
            (
                (dest_hbm, dest),
                (dest_row_hbm, dest_row),
                (offset_hbm, offset),
                (visit_hbm, visit),
                (flags_hbm, flags),
            )
        )
    ]
    for item in small:
        item.start()
    group = min(8, count)
    loads = []
    for k in range(count // group):
        part = pl.ds(k * group, group)
        loads.append(pltpu.make_async_copy(blocks.at[part, :, pl.ds(0, width)], buf.at[part], sem_in.at[k]))
        loads[-1].start()
    zero[...] = jnp.zeros_like(zero)

    def reset(d, carry):
        cnt[d] = 0
        return carry

    def locate(n, carry):
        d = dest[n]
        rank = cnt[d]
        cnt[d] = rank + 1
        where[n] = rank
        return carry

    def blank(d, carry):
        for r in range(SLOT_CAP):

            @pl.when(cnt[d] <= r)
            def _():
                pltpu.make_async_copy(zero, send.at[d, pl.ds(r * slot_rows, slot_rows)], sem_out).start()

        return carry

    lax.fori_loop(0, sources, reset, 0, unroll=8)
    for item in small:
        item.wait()
    lax.fori_loop(0, count, locate, 0, unroll=4)
    lax.fori_loop(0, sources, blank, 0, unroll=4)
    goal = jnp.broadcast_to(dest_row[...].astype(jnp.float32), (count, count))
    earlier = lax.broadcasted_iota(jnp.int32, (count, count), 0) < lax.broadcasted_iota(jnp.int32, (count, count), 1)
    rank = jnp.sum(jnp.where((jnp.transpose(goal) == goal) & earlier, 1.0, 0.0), axis=0, keepdims=True)
    line = goal[0:1, :] * META_ROWS + rank * 4
    bits = flags[...]
    start = visit[...] * row_count + offset[...] + 1
    row16 = lax.broadcasted_iota(jnp.int32, (BLOCK_ROWS, count), 0)
    start = jnp.broadcast_to(start, (BLOCK_ROWS, count))
    kinds = (
        jnp.bitwise_and(bits, 255),
        jnp.right_shift(bits, 8),
        jnp.where(row16 == 0, jnp.bitwise_and(start, 255), jnp.where(row16 == 1, jnp.right_shift(start, 8), 0)),
    )
    row_id = lax.broadcasted_iota(jnp.int32, (sources * META_ROWS, count), 0).astype(jnp.float32)
    total = jnp.zeros((sources * META_ROWS, BLOCK_ROWS), jnp.float32)
    for t, kind in enumerate(kinds):
        pick = jnp.where(row_id == line + t, 1.0, 0.0).astype(jnp.bfloat16)
        total = total + lax.dot_general(
            pick,
            kind.astype(jnp.float32).astype(jnp.bfloat16),
            (((1,), (1,)), ((), ())),
            preferred_element_type=jnp.float32,
        )
    wide[...] = jnp.zeros_like(wide)
    wide[:, 0:BLOCK_ROWS] = total
    narrow[...] = wide[...].reshape(sources, META_ROWS, 128).astype(jnp.bfloat16)
    label = pltpu.make_async_copy(narrow, send.at[:, pl.ds(data_rows, META_ROWS), :], sem_small.at[len(small)])
    label.start()
    for k in range(count // group):
        loads[k].wait()
        for n in range(k * group, (k + 1) * group):
            word = jnp.broadcast_to(flags[:, n : n + 1], (BLOCK_ROWS, 128))
            for q in range(FIRST):
                good = (1 - jnp.bitwise_and(jnp.right_shift(word, q), 1)).astype(jnp.float32).astype(jnp.bfloat16)
                out[n, q * BLOCK_ROWS : (q + 1) * BLOCK_ROWS, :] = buf[n, :, q * 128 : (q + 1) * 128] * good
            target = send.at[dest[n], pl.ds(pl.multiple_of(where[n] * slot_rows, slot_rows), slot_rows)]
            pltpu.make_async_copy(out.at[n], target, sem_out).start()
    whole = send.at[:, pl.ds(0, data_rows), :]
    pltpu.make_async_copy(whole, whole, sem_out).wait()
    label.wait()


def pack_first(dest, offset, visit_id, flags, blocks, sources, row_count):
    count, _, cols = blocks.shape
    width = cols // GROUPS * FIRST
    hbm = pl.BlockSpec(memory_space=pltpu.HBM)
    slot_rows = FIRST * BLOCK_ROWS

    def kernel(*refs):
        first_kernel(*refs, row_count=row_count)

    return pl.pallas_call(
        kernel,
        out_shape=pltpu.HBM((sources, SLOT_CAP * slot_rows + META_ROWS, 128), jnp.bfloat16),
        in_specs=[hbm] * 6,
        out_specs=hbm,
        scratch_shapes=[
            pltpu.VMEM((1, count), jnp.int32),
            pltpu.VMEM((1, count), jnp.int32),
            pltpu.VMEM((1, count), jnp.int32),
            pltpu.VMEM((BLOCK_ROWS, count), jnp.int32),
            pltpu.SMEM((count,), jnp.int32),
            pltpu.VMEM((count, BLOCK_ROWS, width), jnp.bfloat16),
            pltpu.VMEM((count, slot_rows, 128), jnp.bfloat16),
            pltpu.VMEM((slot_rows, 128), jnp.bfloat16),
            pltpu.VMEM((sources * META_ROWS, 128), jnp.float32),
            pltpu.VMEM((sources, META_ROWS, 128), jnp.bfloat16),
            pltpu.SMEM((sources,), jnp.int32),
            pltpu.SMEM((count,), jnp.int32),
            pltpu.SemaphoreType.DMA((6,)),
            pltpu.SemaphoreType.DMA((max(1, count // 8),)),
            pltpu.SemaphoreType.DMA,
        ],
        compiler_params=params(24),
        name="pack_first_groups",
    )(
        *(
            pltpu.with_memory_space_constraint(item, pltpu.HBM)
            for item in (dest[None, :], offset[None, :], visit_id[None, :], flags, dest, blocks)
        )
    )


def pack_kernel(dest_hbm, bad_hbm, blocks, send, dest, bad, buf, out, zero, spread, cnt, where, sem_small, sem_in, sem_out):
    count = blocks.shape[0]
    cols = send.shape[2]
    skip = blocks.shape[2] - cols
    slots = send.shape[0]
    group = min(8, count)
    small = [
        pltpu.make_async_copy(dest_hbm, dest, sem_small.at[0]),
        pltpu.make_async_copy(bad_hbm, bad, sem_small.at[1]),
    ]
    for item in small:
        item.start()
    for k in range(count // group):
        part = pl.ds(k * group, group)
        pltpu.make_async_copy(blocks.at[part, :, pl.ds(skip, cols)], buf.at[part], sem_in.at[k]).start()

    def reset(d, carry):
        cnt[d] = 0
        return carry

    def locate(n, carry):
        d = dest[n]
        rank = cnt[d]
        cnt[d] = rank + 1
        where[n] = d * SLOT_CAP + rank
        return carry

    def blank(d, carry):
        for r in range(SLOT_CAP):

            @pl.when(cnt[d] <= r)
            def _():
                pltpu.make_async_copy(zero, send.at[d * SLOT_CAP + r], sem_out).start()

        return carry

    zero[...] = jnp.zeros_like(zero)
    lax.fori_loop(0, slots // SLOT_CAP, reset, 0, unroll=8)
    for item in small:
        item.wait()
    lax.fori_loop(0, count, locate, 0, unroll=4)
    lax.fori_loop(0, slots // SLOT_CAP, blank, 0, unroll=4)
    row_id = lax.broadcasted_iota(jnp.int32, (128, 128), 0)
    for q in range(cols // 128):
        spread[:, q * 128 : (q + 1) * 128] = jnp.where(row_id == FIRST + q, 1.0, 0.0).astype(jnp.bfloat16)
    flags = bad[...]
    lane = lax.broadcasted_iota(jnp.int32, (BLOCK_ROWS, 128), 1)
    shift = jnp.minimum(lane, GROUPS)
    for k in range(count // group):
        rows = []
        for n in range(k * group, (k + 1) * group):
            word = jnp.broadcast_to(flags[:, n : n + 1], (BLOCK_ROWS, 128))
            bit = jnp.bitwise_and(jnp.right_shift(word, shift), 1)
            rows.append((1 - bit).astype(jnp.float32))
        good = jnp.concatenate(rows, axis=0).astype(jnp.bfloat16)
        mask = jnp.dot(good, spread[...], preferred_element_type=jnp.float32).astype(jnp.bfloat16)
        part = pl.ds(k * group, group)
        pltpu.make_async_copy(blocks.at[part, :, pl.ds(skip, cols)], buf.at[part], sem_in.at[k]).wait()
        out[part] = buf[part] * mask.reshape(group, BLOCK_ROWS, cols)
        for n in range(k * group, (k + 1) * group):
            pltpu.make_async_copy(out.at[n], send.at[where[n]], sem_out).start()
    pltpu.make_async_copy(send, send, sem_out).wait()


def pack(dest, flags, blocks, slots):
    count, _, cols = blocks.shape
    cols = cols - cols // GROUPS * FIRST
    hbm = pl.BlockSpec(memory_space=pltpu.HBM)
    return pl.pallas_call(
        pack_kernel,
        out_shape=pltpu.HBM((slots, BLOCK_ROWS, cols), jnp.bfloat16),
        in_specs=[hbm, hbm, hbm],
        out_specs=hbm,
        scratch_shapes=[
            pltpu.SMEM((count,), jnp.int32),
            pltpu.VMEM((BLOCK_ROWS, count), jnp.int32),
            pltpu.VMEM((count, BLOCK_ROWS, cols), jnp.bfloat16),
            pltpu.VMEM((count, BLOCK_ROWS, cols), jnp.bfloat16),
            pltpu.VMEM((BLOCK_ROWS, cols), jnp.bfloat16),
            pltpu.VMEM((128, cols), jnp.bfloat16),
            pltpu.SMEM((slots // SLOT_CAP,), jnp.int32),
            pltpu.SMEM((count,), jnp.int32),
            pltpu.SemaphoreType.DMA((2,)),
            pltpu.SemaphoreType.DMA((max(1, count // 8),)),
            pltpu.SemaphoreType.DMA,
        ],
        compiler_params=params(24),
        name="pack_blocks",
    )(*(pltpu.with_memory_space_constraint(item, pltpu.HBM) for item in (dest, flags, blocks)))


def cover_kernel(got, placing, spread, factor, meta, sem):
    sources = got.shape[0]
    slots = sources * SLOT_CAP
    label = pltpu.make_async_copy(got.at[:, pl.ds(got.shape[1] - META_ROWS, META_ROWS), :], meta, sem)
    label.start()
    label.wait()
    cols = spread.shape[1]
    lines = placing.shape[1]
    rows = placing.shape[0]
    turned = jnp.transpose(meta[...].astype(jnp.float32).reshape(sources * META_ROWS, 128))
    turned = turned[0:BLOCK_ROWS, :].astype(jnp.bfloat16)
    meta_row = lax.broadcasted_iota(jnp.int32, (sources * META_ROWS, slots), 0)
    meta_slot = lax.broadcasted_iota(jnp.int32, (sources * META_ROWS, slots), 1)
    meta_base = meta_slot // SLOT_CAP * META_ROWS + meta_slot % SLOT_CAP * 4
    low, high, begin = (
        jnp.dot(
            turned,
            jnp.where(meta_row == meta_base + t, 1.0, 0.0).astype(jnp.bfloat16),
            preferred_element_type=jnp.float32,
        )
        for t in range(3)
    )
    begin = jnp.broadcast_to(begin[0:1, :] + 256.0 * begin[1:2, :] - 1.0, (8, slots))
    words = jnp.concatenate([low + 256.0 * high, begin], axis=0)
    slot_id = lax.broadcasted_iota(jnp.int32, (slots, lines), 0)
    line_id = lax.broadcasted_iota(jnp.int32, (slots, lines), 1)
    pick = jnp.where(slot_id == line_id // BLOCK_ROWS, 1.0, 0.0).astype(jnp.float32)
    wide = jnp.dot(words, pick, precision=lax.Precision.HIGHEST, preferred_element_type=jnp.float32)
    lane = lax.broadcasted_iota(jnp.int32, (1, lines), 1)
    inner = lane % BLOCK_ROWS
    start = wide[BLOCK_ROWS : BLOCK_ROWS + 1, :].astype(jnp.int32)
    target = jnp.where(start >= 0, start + inner, -1)
    own = lax.broadcasted_iota(jnp.int32, (BLOCK_ROWS, lines), 0) == inner
    word = jnp.sum(jnp.where(own, wide[0:BLOCK_ROWS, :], 0.0), axis=0, keepdims=True).astype(jnp.int32)
    group = lax.broadcasted_iota(jnp.int32, (128, lines), 0)
    bit = jnp.bitwise_and(jnp.right_shift(jnp.broadcast_to(word, (128, lines)), jnp.minimum(group, GROUPS)), 1)
    good = (1 - bit).astype(jnp.float32).astype(jnp.bfloat16)
    step = 128
    for k in range(rows // step):
        row = lax.broadcasted_iota(jnp.int32, (step, lines), 0) + k * step
        placing[k * step : (k + 1) * step, :] = jnp.where(row == target, 1.0, 0.0).astype(jnp.bfloat16)
    counted = lax.dot_general(placing[...], good, (((1,), (1,)), ((), ())), preferred_element_type=jnp.float32)
    factor[...] = jnp.minimum(counted, 1.0) / jnp.maximum(counted, 1.0)
    wide_group = cols // GROUPS
    for q in range(GROUPS):
        spread[:, q * wide_group : (q + 1) * wide_group] = jnp.broadcast_to(
            counted[:, q : q + 1], (rows, wide_group)
        ).astype(jnp.bfloat16)


def cover(got, row_count, cols):
    sources = got.shape[0]
    slots = sources * SLOT_CAP
    vmem = pl.BlockSpec(memory_space=pltpu.VMEM)
    return pl.pallas_call(
        cover_kernel,
        out_shape=(
            jax.ShapeDtypeStruct((VISITS * row_count, slots * BLOCK_ROWS), jnp.bfloat16),
            jax.ShapeDtypeStruct((VISITS * row_count, cols), jnp.bfloat16),
            jax.ShapeDtypeStruct((VISITS * row_count, 128), jnp.float32),
        ),
        in_specs=[pl.BlockSpec(memory_space=pltpu.HBM)],
        out_specs=(vmem, vmem, vmem),
        scratch_shapes=[pltpu.VMEM((sources, META_ROWS, 128), jnp.bfloat16), pltpu.SemaphoreType.DMA],
        compiler_params=params(24),
        name="coverage",
    )(pltpu.with_memory_space_constraint(got, pltpu.HBM))


def column_kernel(padded, table, out):
    for k in range(out.shape[2] // 128):
        window = padded[:, k * 128 : k * 128 + 256]
        result = jnp.dot(window, table[...], preferred_element_type=jnp.float32)
        for j in range(NPOW):
            out[j, :, k * 128 : (k + 1) * 128] = result[:, j * 128 : (j + 1) * 128].astype(jnp.bfloat16)


def column_pass(padded, taps, cols):
    rows = padded.shape[0]
    vmem = pl.BlockSpec(memory_space=pltpu.VMEM)
    table = jnp.asarray(column_table(taps).astype(ml_dtypes.bfloat16))
    return pl.pallas_call(
        column_kernel,
        out_shape=jax.ShapeDtypeStruct((NPOW, rows, cols), jnp.bfloat16),
        in_specs=[vmem, vmem],
        out_specs=vmem,
        compiler_params=params(24),
        name="column_pass",
    )(padded, table)


GRAM_ROWS = 240


def gram_kernel(images, table, count, out, stage, acc):
    cols = images.shape[2]
    rows = count.shape[0] // VISITS
    chunk = stage.shape[1]
    ones = jnp.ones((8, chunk), jnp.float32)
    blank = jnp.zeros((8, chunk), jnp.float32)
    acc[...] = jnp.zeros_like(acc)

    def tile(step, carry):
        first = pl.multiple_of(step * TILE, TILE)
        for k in range(cols // chunk):
            lanes = slice(k * chunk, (k + 1) * chunk)
            at = 0
            for j in range(NPOW):
                size = TILE * (NPOW - j)
                window = images[j, pl.ds(first, SPAN), lanes]
                stage[at : at + size, :] = jnp.dot(
                    table[at : at + size, :], window, preferred_element_type=jnp.float32
                )
                at += size
            for pair in range(TILE // 16):
                seen = [
                    jnp.minimum(
                        count[pl.ds(pl.multiple_of(v * rows + first + pair * 16, 16), 16), lanes].astype(jnp.float32), 1.0
                    )
                    for v in range(VISITS)
                ]
                for half in range(2):
                    cb = pair * 2 + half
                    pieces = []
                    at = 0
                    for j in range(NPOW):
                        size = 8 * (NPOW - j)
                        pieces.append(stage[at + cb * size : at + (cb + 1) * size, :])
                        at += TILE * (NPOW - j)
                    basis = jnp.concatenate(pieces + [ones, blank], axis=0)
                    scaled = []
                    for v in range(VISITS):
                        w = seen[v][half * 8 : half * 8 + 8]
                        scaled.append(
                            (basis.reshape(GRAM_ROWS // 8, 8, chunk) * w[None])
                            .reshape(GRAM_ROWS, chunk)
                            .astype(jnp.bfloat16)
                        )
                    acc[...] += lax.dot_general(
                        jnp.concatenate(scaled, axis=0),
                        basis.astype(jnp.bfloat16),
                        (((1,), (1,)), ((), ())),
                        preferred_element_type=jnp.float32,
                    )
        return carry

    lax.fori_loop(0, rows // TILE, tile, 0)
    row_id = lax.broadcasted_iota(jnp.int32, (GRAM_ROWS, GRAM_ROWS), 0)
    lane_id = lax.broadcasted_iota(jnp.int32, (GRAM_ROWS, GRAM_ROWS), 1)
    same = (row_id % 8) == (lane_id % 8)
    gather = jnp.where(
        lax.broadcasted_iota(jnp.int32, (GRAM_ROWS, 128), 0) // 8
        == lax.broadcasted_iota(jnp.int32, (GRAM_ROWS, 128), 1),
        1.0,
        0.0,
    )
    for v in range(VISITS):
        kept = jnp.where(same, acc[v * GRAM_ROWS : (v + 1) * GRAM_ROWS, :], 0.0)
        kept = jnp.sum(kept.reshape(GRAM_ROWS // 8, 8, GRAM_ROWS), axis=1)
        full = jnp.dot(kept, gather, precision=lax.Precision.HIGHEST, preferred_element_type=jnp.float32)
        out[v] = full[:TERMS, :TERMS]


def gram(images, count, taps):
    vmem = pl.BlockSpec(memory_space=pltpu.VMEM)
    table = jnp.asarray(row_table(taps).astype(ml_dtypes.bfloat16))
    return pl.pallas_call(
        gram_kernel,
        out_shape=jax.ShapeDtypeStruct((VISITS, TERMS, TERMS), jnp.float32),
        in_specs=[vmem, vmem, vmem],
        out_specs=vmem,
        scratch_shapes=[
            pltpu.VMEM((BASIS_COUNT * TILE, 1024), jnp.float32),
            pltpu.VMEM((VISITS * GRAM_ROWS, GRAM_ROWS), jnp.float32),
        ],
        compiler_params=params(28),
        name="normal_matrix",
    )(images, table, count)


ONES_ROWS = 16
PLACE_CHUNK = 512


def scale_rows(summed, factor, first, group):
    rows = summed.shape[0]
    spread = jnp.concatenate(
        [
            jnp.broadcast_to(factor[:, first + q : first + q + 1], (rows, group))
            for q in range(summed.shape[1] // group)
        ],
        axis=1,
    )
    return (summed * spread).astype(jnp.bfloat16)


def correlate(value, images, lanes, rows, partial):
    chunk = value.shape[1]
    ones = jnp.ones((ONES_ROWS, chunk), jnp.bfloat16)
    for t in range(rows // TILE):
        left = jnp.concatenate(
            [value[v * rows + t * TILE : v * rows + (t + 1) * TILE, :] for v in range(VISITS)], axis=0
        )
        right = images[:, t * TILE : t * TILE + SPAN, lanes].reshape(NPOW * SPAN, chunk)
        right = jnp.concatenate([right, ones], axis=0)
        product = lax.dot_general(left, right, (((1,), (1,)), ((), ())), preferred_element_type=jnp.float32)
        partial = product if partial is None else partial + product
    return partial


def early_kernel(got, placing, factor, images, science, acc, buf, sem):
    rows = science.shape[1]
    copy = pltpu.make_async_copy(got.at[:, pl.ds(0, buf.shape[1]), :], buf, sem)
    copy.start()
    copy.wait()
    columns = []
    for q in range(FIRST):
        ranks = [
            buf[:, (r * FIRST + q) * BLOCK_ROWS : (r * FIRST + q + 1) * BLOCK_ROWS, :] for r in range(SLOT_CAP)
        ]
        columns.append(jnp.stack(ranks, axis=1).reshape(-1, 128))
    right = jnp.concatenate(columns, axis=1)
    summed = jnp.dot(placing[...], right, preferred_element_type=jnp.float32)
    value = scale_rows(summed, factor, 0, 128)
    for v in range(VISITS):
        science[v, :, :] = value[v * rows : (v + 1) * rows, :]
    acc[...] = correlate(value, images, slice(0, FIRST * 128), rows, None)


def place_early(got, placing, factor, images, row_count):
    sources = got.shape[0]
    vmem = pl.BlockSpec(memory_space=pltpu.VMEM)
    return pl.pallas_call(
        early_kernel,
        out_shape=(
            jax.ShapeDtypeStruct((VISITS, row_count, FIRST * 128), jnp.bfloat16),
            jax.ShapeDtypeStruct((VISITS * TILE, NPOW * SPAN + ONES_ROWS), jnp.float32),
        ),
        in_specs=[pl.BlockSpec(memory_space=pltpu.HBM), vmem, vmem, vmem],
        out_specs=(vmem, vmem),
        scratch_shapes=[
            pltpu.VMEM((sources, SLOT_CAP * FIRST * BLOCK_ROWS, 128), jnp.bfloat16),
            pltpu.SemaphoreType.DMA,
        ],
        compiler_params=params(28),
        name="place_first_groups",
    )(pltpu.with_memory_space_constraint(got, pltpu.HBM), placing, factor, images)


def place_kernel(got, placing, factor_hbm, source, table_hbm, before_hbm, science, sums, images, buf, acc, factor, table, before, sem_got, sem_img, sem_small):
    rows = science.shape[1]
    cols = science.shape[2]
    skip = source.shape[2] - cols
    chunk = PLACE_CHUNK
    group = source.shape[2] // GROUPS
    small = pltpu.make_async_copy(factor_hbm, factor, sem_small.at[0])
    small.start()
    later = [
        pltpu.make_async_copy(before_hbm, before, sem_small.at[1]),
        pltpu.make_async_copy(table_hbm, table, sem_small.at[2]),
    ]
    rest = pltpu.make_async_copy(source.at[:, :, pl.ds(0, skip)], images.at[:, :, pl.ds(0, skip)], sem_img.at[cols // chunk])
    copies = []
    for c in range(cols // chunk):
        lanes = slice(c * chunk, (c + 1) * chunk)
        late = slice(skip + c * chunk, skip + (c + 1) * chunk)
        copies.append(
            (
                pltpu.make_async_copy(got.at[:, :, lanes], buf.at[:, :, lanes], sem_got.at[c]),
                pltpu.make_async_copy(source.at[:, :, late], images.at[:, :, late], sem_img.at[c]),
            )
        )
    for pair in copies[:2]:
        for item in pair:
            item.start()
    partial = None
    for c in range(cols // chunk):
        lanes = slice(c * chunk, (c + 1) * chunk)
        late = slice(skip + c * chunk, skip + (c + 1) * chunk)
        copies[c][0].wait()
        if c + 2 < len(copies):
            copies[c + 2][0].start()
        summed = jnp.dot(placing[...], buf[:, :, lanes].reshape(-1, chunk), preferred_element_type=jnp.float32)
        if c == 0:
            small.wait()
            for item in later:
                item.start()
        value = scale_rows(summed, factor, (skip + c * chunk) // group, group)
        for v in range(VISITS):
            science[v, :, lanes] = value[v * rows : (v + 1) * rows, :]
        copies[c][1].wait()
        if c + 2 < len(copies):
            copies[c + 2][1].start()
        if c == len(copies) - 2:
            rest.start()
        partial = correlate(value, images, late, rows, partial)
    for item in later:
        item.wait()
    acc[...] = partial + before[...]
    row_id = lax.broadcasted_iota(jnp.int32, (32, 128), 0)
    lane_id = lax.broadcasted_iota(jnp.int32, (32, 128), 1)
    result = jnp.zeros((32, 128), jnp.float32)
    for v in range(VISITS):
        parts = []
        for j in range(NPOW):
            cross = acc[v * TILE : (v + 1) * TILE, j * SPAN : (j + 1) * SPAN]
            for i in range(NPOW - j):
                parts.append(jnp.sum(cross * table[i], axis=0, keepdims=True))
        parts.append(jnp.zeros((32 - BASIS_COUNT, SPAN), jnp.float32))
        item = jnp.sum(jnp.concatenate(parts, axis=0), axis=1, keepdims=True)
        flat = jnp.sum(acc[v * TILE : (v + 1) * TILE, NPOW * SPAN : NPOW * SPAN + 1], axis=0, keepdims=True)
        item = jnp.where(row_id == BASIS_COUNT, flat, item)
        result = result + jnp.where(lane_id == v, item, 0.0)
    sums[...] = result
    rest.wait()


def place(got, placing, factor, images, bands, before, row_count):
    slots, _, cols = got.shape
    table = jnp.asarray(bands)
    vmem = pl.BlockSpec(memory_space=pltpu.VMEM)
    hbm = pl.BlockSpec(memory_space=pltpu.HBM)
    return pl.pallas_call(
        place_kernel,
        out_shape=(
            jax.ShapeDtypeStruct((VISITS, row_count, cols), jnp.bfloat16),
            jax.ShapeDtypeStruct((32, 128), jnp.float32),
            jax.ShapeDtypeStruct(images.shape, jnp.bfloat16),
        ),
        in_specs=[hbm, vmem, hbm, hbm, hbm, hbm],
        out_specs=(vmem, vmem, vmem),
        scratch_shapes=[
            pltpu.VMEM(got.shape, jnp.bfloat16),
            pltpu.VMEM((VISITS * TILE, NPOW * SPAN + ONES_ROWS), jnp.float32),
            pltpu.VMEM(factor.shape, jnp.float32),
            pltpu.VMEM(table.shape, jnp.float32),
            pltpu.VMEM(before.shape, jnp.float32),
            pltpu.SemaphoreType.DMA((cols // PLACE_CHUNK,)),
            pltpu.SemaphoreType.DMA((cols // PLACE_CHUNK + 1,)),
            pltpu.SemaphoreType.DMA((3,)),
        ],
        compiler_params=params(40),
        name="place_and_correlate",
    )(
        pltpu.with_memory_space_constraint(got, pltpu.HBM),
        placing,
        pltpu.with_memory_space_constraint(factor, pltpu.HBM),
        pltpu.with_memory_space_constraint(images, pltpu.HBM),
        pltpu.with_memory_space_constraint(table, pltpu.HBM),
        pltpu.with_memory_space_constraint(before, pltpu.HBM),
    )


def model_kernel(sums, inverse, table, images, early, science, count, out, coeffs, wide, narrow, buf, sem):
    rows = science.shape[1]
    skip = early.shape[2]
    cols = skip + science.shape[2]
    chunk = 256
    rhs = sums[0:32, :]
    for k in range(1, sums.shape[0] // 32):
        rhs = rhs + sums[k * 32 : (k + 1) * 32, :]
    level = []
    for v in range(VISITS):
        row = jnp.sum(inverse[v] * rhs[:, v : v + 1], axis=0, keepdims=True)
        coeffs[v : v + 1, :] = row[:, :TERMS]
        level.append(row[:, BASIS_COUNT : BASIS_COUNT + 1])
        index = 0
        for j in range(NPOW):
            kernel = jnp.zeros((TILE, SPAN), jnp.float32)
            for i in range(NPOW - j):
                kernel = kernel + row[:, index : index + 1] * table[i]
                index += 1
            wide[v * TILE : (v + 1) * TILE, j * SPAN : (j + 1) * SPAN] = kernel
    narrow[...] = wide[...].astype(jnp.bfloat16)
    copies = []
    for c in range(cols // chunk):
        lanes = slice(c * chunk, (c + 1) * chunk)
        for t in range(rows // TILE):
            right = images[:, t * TILE : t * TILE + SPAN, lanes].reshape(NPOW * SPAN, chunk)
            model = jnp.dot(narrow[...], right, preferred_element_type=jnp.float32)
            for v in range(VISITS):
                at = slice(t * TILE, (t + 1) * TILE)
                full = model[v * TILE : (v + 1) * TILE, :] + level[v]
                seen = count[v * rows + t * TILE : v * rows + (t + 1) * TILE, lanes]
                weight = jnp.minimum(seen.astype(jnp.float32), 1.0)
                if (c + 1) * chunk <= skip:
                    seen = early[v, at, lanes]
                else:
                    seen = science[v, at, c * chunk - skip : (c + 1) * chunk - skip]
                buf[v, at, lanes] = (seen.astype(jnp.float32) - weight * full).astype(jnp.bfloat16)
        copies.append(pltpu.make_async_copy(buf.at[:, :, lanes], out.at[:, :, lanes], sem.at[c]))
        copies[-1].start()
    for item in copies:
        item.wait()


def model(sums, inverse, images, early, science, count, bands):
    _, rows, cols = science.shape
    cols = cols + early.shape[2]
    table = jnp.asarray(bands)
    vmem = pl.BlockSpec(memory_space=pltpu.VMEM)
    return pl.pallas_call(
        model_kernel,
        out_shape=(
            pltpu.HBM((VISITS, rows, cols), jnp.bfloat16),
            jax.ShapeDtypeStruct((VISITS, TERMS), jnp.float32),
        ),
        in_specs=[vmem] * 7,
        out_specs=(pl.BlockSpec(memory_space=pltpu.HBM), vmem),
        scratch_shapes=[
            pltpu.VMEM((VISITS * TILE, NPOW * SPAN), jnp.float32),
            pltpu.VMEM((VISITS * TILE, NPOW * SPAN), jnp.bfloat16),
            pltpu.VMEM((VISITS, rows, cols), jnp.bfloat16),
            pltpu.SemaphoreType.DMA((cols // 256,)),
        ],
        compiler_params=params(28),
        name="model_and_difference",
    )(sums, inverse, table, images, early, science, count)


def inverse_of(matrix):
    eye = jnp.broadcast_to(jnp.eye(TERMS, dtype=jnp.float32), matrix.shape)
    lower = jnp.linalg.cholesky(matrix)
    half = jax.scipy.linalg.solve_triangular(lower, eye, lower=True)
    return jnp.einsum("vkb,vkc->vbc", half, half, precision=lax.Precision.HIGHEST)


def halo(rows):
    count = lax.axis_size("visit")
    up = [(i, i + 1) for i in range(count - 1)]
    down = [(i + 1, i) for i in range(count - 1)]
    above = lax.ppermute(rows[-MARGIN:], "visit", up)
    below = lax.ppermute(rows[:MARGIN], "visit", down)
    return above, below


def body(template, blocks, dest, offset, visit_id, badmask):
    row_count = template.shape[1]
    cols = template.shape[2]
    axes = ("patch", "visit")
    sources = lax.axis_size("patch") * lax.axis_size("visit")
    slots = sources * SLOT_CAP
    taps = taps_table()
    bands = row_bands(taps)

    flags = badmask.T
    send_first = pack_first(dest, offset, visit_id, flags, blocks, sources, row_count)
    send_first, rows = lax.optimization_barrier((send_first, template[0]))
    got_first = lax.all_to_all(send_first, axes, split_axis=0, concat_axis=0, tiled=True)
    got_first = pltpu.with_memory_space_constraint(got_first, pltpu.HBM)
    send = pack(dest, flags, blocks, slots)
    above, below = halo(rows)
    tall = jnp.concatenate([above, rows, below], axis=0)
    padded = jnp.pad(tall, ((0, 0), (HALF_TAPS, 128 - HALF_TAPS)))
    images = column_pass(padded, taps, cols)
    send, got_first, images = lax.optimization_barrier((send, got_first, images))
    got = lax.all_to_all(send, axes, split_axis=0, concat_axis=0, tiled=True)

    placing, count, factor = cover(got_first, row_count, cols)

    shares = lax.all_gather(gram(images, count, taps), "visit", axis=0, tiled=False)
    normal = jnp.sum(shares, axis=0)
    inverse = jnp.pad(inverse_of(normal), ((0, 0), (0, 32 - TERMS), (0, 128 - TERMS)))

    early, before = place_early(got_first, placing, factor, images, row_count)
    science, sums, images = place(got, placing, factor, images, bands, before, row_count)
    sums = lax.all_gather(sums, "visit", axis=0, tiled=True)
    difference, coeffs = model(sums, inverse, images, early, science, count, bands)
    return (difference[:, None], coeffs[:, None])


def solution(mesh):
    in_specs = (
        P("patch", "visit", None),
        P(("patch", "visit"), None, None),
        P(("patch", "visit")),
        P(("patch", "visit")),
        P(("patch", "visit")),
        P(("patch", "visit"), None),
    )
    out_specs = (P(None, "patch", "visit", None), P(None, "patch", None))
    return jax.shard_map(body, mesh=mesh, in_specs=in_specs, out_specs=out_specs, check_vma=False)
```

```python
import jax
import jax.numpy as jnp
import ml_dtypes
import numpy as np
from jax import lax
from jax.experimental import pallas as pl
from jax.experimental.pallas import tpu as pltpu
from jax.sharding import PartitionSpec as P

BLOCK_ROWS = 16
SLOT_CAP = 2
HALF_TAPS = 10
NTAPS = 2 * HALF_TAPS + 1
DEGREE = 6
NPOW = DEGREE + 1
VISITS = 2
BASIS_COUNT = 28
TERMS = 29
GROUPS = 16
TILE = 64
SPAN = 96
SIGMA = 2.0
MARGIN = 16
MIB = 1 << 20


def taps_table():
    places = np.arange(-HALF_TAPS, HALF_TAPS + 1) * 1.0
    basis_rows = []
    for exponent in range(NPOW):
        vector = places**exponent * np.exp(-(places**2) / (2.0 * SIGMA**2))
        for earlier in basis_rows:
            vector = vector - np.dot(earlier, vector) * earlier
        vector = vector / np.sqrt(np.dot(vector, vector))
        basis_rows.append(vector)
    table = np.stack(basis_rows).astype(np.float32)
    return table.astype(ml_dtypes.bfloat16).astype(np.float32)


def band(taps_row, count_out, count_in, shift=0):
    out = np.zeros((count_out, count_in), np.float32)
    for row in range(count_out):
        out[row, row + shift : row + shift + NTAPS] = taps_row
    return out


def column_table(taps):
    return np.concatenate([band(taps[j], 128, 256).T for j in range(NPOW)], axis=1)


def row_bands(taps):
    return np.stack([band(taps[i], TILE, SPAN, MARGIN - HALF_TAPS) for i in range(NPOW)])


def row_table(taps):
    bands = row_bands(taps)
    bands = bands.reshape(NPOW, TILE // 8, 8, SPAN)
    pieces = []
    for j in range(NPOW):
        pieces.append(bands[: NPOW - j].transpose(1, 0, 2, 3).reshape(-1, SPAN))
    return np.concatenate(pieces, axis=0)


def params(mib):
    return pltpu.CompilerParams(vmem_limit_bytes=mib * MIB)


FIRST = 4
META_ROWS = 8


def first_kernel(dest_row_hbm, offset_hbm, visit_hbm, flags_hbm, dest_hbm, blocks, send, dest_row, offset, visit, flags, dest, buf, out, zero, wide, narrow, cnt, where, sem_small, sem_in, sem_out, row_count):
    count = blocks.shape[0]
    sources = send.shape[0]
    data_rows = SLOT_CAP * FIRST * BLOCK_ROWS
    slot_rows = FIRST * BLOCK_ROWS
    width = buf.shape[2]
    small = [
        pltpu.make_async_copy(source, target, sem_small.at[k])
        for k, (source, target) in enumerate(
            (
                (dest_hbm, dest),
                (dest_row_hbm, dest_row),
                (offset_hbm, offset),
                (visit_hbm, visit),
                (flags_hbm, flags),
            )
        )
    ]
    for item in small:
        item.start()
    group = min(8, count)
    loads = []
    for k in range(count // group):
        part = pl.ds(k * group, group)
        loads.append(pltpu.make_async_copy(blocks.at[part, :, pl.ds(0, width)], buf.at[part], sem_in.at[k]))
        loads[-1].start()
    zero[...] = jnp.zeros_like(zero)

    def reset(d, carry):
        cnt[d] = 0
        return carry

    def locate(n, carry):
        d = dest[n]
        rank = cnt[d]
        cnt[d] = rank + 1
        where[n] = rank
        return carry

    def blank(d, carry):
        for r in range(SLOT_CAP):

            @pl.when(cnt[d] <= r)
            def _():
                pltpu.make_async_copy(zero, send.at[d, pl.ds(r * slot_rows, slot_rows)], sem_out).start()

        return carry

    lax.fori_loop(0, sources, reset, 0, unroll=8)
    for item in small:
        item.wait()
    lax.fori_loop(0, count, locate, 0, unroll=4)
    lax.fori_loop(0, sources, blank, 0, unroll=4)
    goal = jnp.broadcast_to(dest_row[...].astype(jnp.float32), (count, count))
    earlier = lax.broadcasted_iota(jnp.int32, (count, count), 0) < lax.broadcasted_iota(jnp.int32, (count, count), 1)
    rank = jnp.sum(jnp.where((jnp.transpose(goal) == goal) & earlier, 1.0, 0.0), axis=0, keepdims=True)
    line = goal[0:1, :] * META_ROWS + rank * 4
    bits = flags[...]
    start = visit[...] * row_count + offset[...] + 1
    row16 = lax.broadcasted_iota(jnp.int32, (BLOCK_ROWS, count), 0)
    start = jnp.broadcast_to(start, (BLOCK_ROWS, count))
    kinds = (
        jnp.bitwise_and(bits, 255),
        jnp.right_shift(bits, 8),
        jnp.where(row16 == 0, jnp.bitwise_and(start, 255), jnp.where(row16 == 1, jnp.right_shift(start, 8), 0)),
    )
    row_id = lax.broadcasted_iota(jnp.int32, (sources * META_ROWS, count), 0).astype(jnp.float32)
    total = jnp.zeros((sources * META_ROWS, BLOCK_ROWS), jnp.float32)
    for t, kind in enumerate(kinds):
        pick = jnp.where(row_id == line + t, 1.0, 0.0).astype(jnp.bfloat16)
        total = total + lax.dot_general(
            pick,
            kind.astype(jnp.float32).astype(jnp.bfloat16),
            (((1,), (1,)), ((), ())),
            preferred_element_type=jnp.float32,
        )
    wide[...] = jnp.zeros_like(wide)
    wide[:, 0:BLOCK_ROWS] = total
    narrow[...] = wide[...].reshape(sources, META_ROWS, 128).astype(jnp.bfloat16)
    label = pltpu.make_async_copy(narrow, send.at[:, pl.ds(data_rows, META_ROWS), :], sem_small.at[len(small)])
    label.start()
    for k in range(count // group):
        loads[k].wait()
        for n in range(k * group, (k + 1) * group):
            word = jnp.broadcast_to(flags[:, n : n + 1], (BLOCK_ROWS, 128))
            for q in range(FIRST):
                good = (1 - jnp.bitwise_and(jnp.right_shift(word, q), 1)).astype(jnp.float32).astype(jnp.bfloat16)
                out[n, q * BLOCK_ROWS : (q + 1) * BLOCK_ROWS, :] = buf[n, :, q * 128 : (q + 1) * 128] * good
            target = send.at[dest[n], pl.ds(pl.multiple_of(where[n] * slot_rows, slot_rows), slot_rows)]
            pltpu.make_async_copy(out.at[n], target, sem_out).start()
    whole = send.at[:, pl.ds(0, data_rows), :]
    pltpu.make_async_copy(whole, whole, sem_out).wait()
    label.wait()


def pack_first(dest, offset, visit_id, flags, blocks, sources, row_count):
    count, _, cols = blocks.shape
    width = cols // GROUPS * FIRST
    hbm = pl.BlockSpec(memory_space=pltpu.HBM)
    slot_rows = FIRST * BLOCK_ROWS

    def kernel(*refs):
        first_kernel(*refs, row_count=row_count)

    return pl.pallas_call(
        kernel,
        out_shape=pltpu.HBM((sources, SLOT_CAP * slot_rows + META_ROWS, 128), jnp.bfloat16),
        in_specs=[hbm] * 6,
        out_specs=hbm,
        scratch_shapes=[
            pltpu.VMEM((1, count), jnp.int32),
            pltpu.VMEM((1, count), jnp.int32),
            pltpu.VMEM((1, count), jnp.int32),
            pltpu.VMEM((BLOCK_ROWS, count), jnp.int32),
            pltpu.SMEM((count,), jnp.int32),
            pltpu.VMEM((count, BLOCK_ROWS, width), jnp.bfloat16),
            pltpu.VMEM((count, slot_rows, 128), jnp.bfloat16),
            pltpu.VMEM((slot_rows, 128), jnp.bfloat16),
            pltpu.VMEM((sources * META_ROWS, 128), jnp.float32),
            pltpu.VMEM((sources, META_ROWS, 128), jnp.bfloat16),
            pltpu.SMEM((sources,), jnp.int32),
            pltpu.SMEM((count,), jnp.int32),
            pltpu.SemaphoreType.DMA((6,)),
            pltpu.SemaphoreType.DMA((max(1, count // 8),)),
            pltpu.SemaphoreType.DMA,
        ],
        compiler_params=params(24),
        name="pack_first_groups",
    )(
        *(
            pltpu.with_memory_space_constraint(item, pltpu.HBM)
            for item in (dest[None, :], offset[None, :], visit_id[None, :], flags, dest, blocks)
        )
    )


def pack_kernel(dest_hbm, bad_hbm, blocks, send, dest, bad, buf, out, zero, spread, cnt, where, sem_small, sem_in, sem_out):
    count = blocks.shape[0]
    cols = send.shape[2]
    skip = blocks.shape[2] - cols
    slots = send.shape[0]
    group = min(8, count)
    small = [
        pltpu.make_async_copy(dest_hbm, dest, sem_small.at[0]),
        pltpu.make_async_copy(bad_hbm, bad, sem_small.at[1]),
    ]
    for item in small:
        item.start()
    for k in range(count // group):
        part = pl.ds(k * group, group)
        pltpu.make_async_copy(blocks.at[part, :, pl.ds(skip, cols)], buf.at[part], sem_in.at[k]).start()

    def reset(d, carry):
        cnt[d] = 0
        return carry

    def locate(n, carry):
        d = dest[n]
        rank = cnt[d]
        cnt[d] = rank + 1
        where[n] = d * SLOT_CAP + rank
        return carry

    def blank(d, carry):
        for r in range(SLOT_CAP):

            @pl.when(cnt[d] <= r)
            def _():
                pltpu.make_async_copy(zero, send.at[d * SLOT_CAP + r], sem_out).start()

        return carry

    zero[...] = jnp.zeros_like(zero)
    lax.fori_loop(0, slots // SLOT_CAP, reset, 0, unroll=8)
    for item in small:
        item.wait()
    lax.fori_loop(0, count, locate, 0, unroll=4)
    lax.fori_loop(0, slots // SLOT_CAP, blank, 0, unroll=4)
    row_id = lax.broadcasted_iota(jnp.int32, (128, 128), 0)
    for q in range(cols // 128):
        spread[:, q * 128 : (q + 1) * 128] = jnp.where(row_id == FIRST + q, 1.0, 0.0).astype(jnp.bfloat16)
    flags = bad[...]
    lane = lax.broadcasted_iota(jnp.int32, (BLOCK_ROWS, 128), 1)
    shift = jnp.minimum(lane, GROUPS)
    for k in range(count // group):
        rows = []
        for n in range(k * group, (k + 1) * group):
            word = jnp.broadcast_to(flags[:, n : n + 1], (BLOCK_ROWS, 128))
            bit = jnp.bitwise_and(jnp.right_shift(word, shift), 1)
            rows.append((1 - bit).astype(jnp.float32))
        good = jnp.concatenate(rows, axis=0).astype(jnp.bfloat16)
        mask = jnp.dot(good, spread[...], preferred_element_type=jnp.float32).astype(jnp.bfloat16)
        part = pl.ds(k * group, group)
        pltpu.make_async_copy(blocks.at[part, :, pl.ds(skip, cols)], buf.at[part], sem_in.at[k]).wait()
        out[part] = buf[part] * mask.reshape(group, BLOCK_ROWS, cols)
        for n in range(k * group, (k + 1) * group):
            pltpu.make_async_copy(out.at[n], send.at[where[n]], sem_out).start()
    pltpu.make_async_copy(send, send, sem_out).wait()


def pack(dest, flags, blocks, slots):
    count, _, cols = blocks.shape
    cols = cols - cols // GROUPS * FIRST
    hbm = pl.BlockSpec(memory_space=pltpu.HBM)
    return pl.pallas_call(
        pack_kernel,
        out_shape=pltpu.HBM((slots, BLOCK_ROWS, cols), jnp.bfloat16),
        in_specs=[hbm, hbm, hbm],
        out_specs=hbm,
        scratch_shapes=[
            pltpu.SMEM((count,), jnp.int32),
            pltpu.VMEM((BLOCK_ROWS, count), jnp.int32),
            pltpu.VMEM((count, BLOCK_ROWS, cols), jnp.bfloat16),
            pltpu.VMEM((count, BLOCK_ROWS, cols), jnp.bfloat16),
            pltpu.VMEM((BLOCK_ROWS, cols), jnp.bfloat16),
            pltpu.VMEM((128, cols), jnp.bfloat16),
            pltpu.SMEM((slots // SLOT_CAP,), jnp.int32),
            pltpu.SMEM((count,), jnp.int32),
            pltpu.SemaphoreType.DMA((2,)),
            pltpu.SemaphoreType.DMA((max(1, count // 8),)),
            pltpu.SemaphoreType.DMA,
        ],
        compiler_params=params(24),
        name="pack_blocks",
    )(*(pltpu.with_memory_space_constraint(item, pltpu.HBM) for item in (dest, flags, blocks)))


def cover_kernel(got, placing, spread, factor, meta, sem):
    sources = got.shape[0]
    slots = sources * SLOT_CAP
    label = pltpu.make_async_copy(got.at[:, pl.ds(got.shape[1] - META_ROWS, META_ROWS), :], meta, sem)
    label.start()
    label.wait()
    cols = spread.shape[1]
    lines = placing.shape[1]
    rows = placing.shape[0]
    turned = jnp.transpose(meta[...].astype(jnp.float32).reshape(sources * META_ROWS, 128))
    turned = turned[0:BLOCK_ROWS, :].astype(jnp.bfloat16)
    meta_row = lax.broadcasted_iota(jnp.int32, (sources * META_ROWS, slots), 0)
    meta_slot = lax.broadcasted_iota(jnp.int32, (sources * META_ROWS, slots), 1)
    meta_base = meta_slot // SLOT_CAP * META_ROWS + meta_slot % SLOT_CAP * 4
    low, high, begin = (
        jnp.dot(
            turned,
            jnp.where(meta_row == meta_base + t, 1.0, 0.0).astype(jnp.bfloat16),
            preferred_element_type=jnp.float32,
        )
        for t in range(3)
    )
    begin = jnp.broadcast_to(begin[0:1, :] + 256.0 * begin[1:2, :] - 1.0, (8, slots))
    words = jnp.concatenate([low + 256.0 * high, begin], axis=0)
    slot_id = lax.broadcasted_iota(jnp.int32, (slots, lines), 0)
    line_id = lax.broadcasted_iota(jnp.int32, (slots, lines), 1)
    pick = jnp.where(slot_id == line_id // BLOCK_ROWS, 1.0, 0.0).astype(jnp.float32)
    wide = jnp.dot(words, pick, precision=lax.Precision.HIGHEST, preferred_element_type=jnp.float32)
    lane = lax.broadcasted_iota(jnp.int32, (1, lines), 1)
    inner = lane % BLOCK_ROWS
    start = wide[BLOCK_ROWS : BLOCK_ROWS + 1, :].astype(jnp.int32)
    target = jnp.where(start >= 0, start + inner, -1)
    own = lax.broadcasted_iota(jnp.int32, (BLOCK_ROWS, lines), 0) == inner
    word = jnp.sum(jnp.where(own, wide[0:BLOCK_ROWS, :], 0.0), axis=0, keepdims=True).astype(jnp.int32)
    group = lax.broadcasted_iota(jnp.int32, (128, lines), 0)
    bit = jnp.bitwise_and(jnp.right_shift(jnp.broadcast_to(word, (128, lines)), jnp.minimum(group, GROUPS)), 1)
    good = (1 - bit).astype(jnp.float32).astype(jnp.bfloat16)
    step = 128
    for k in range(rows // step):
        row = lax.broadcasted_iota(jnp.int32, (step, lines), 0) + k * step
        placing[k * step : (k + 1) * step, :] = jnp.where(row == target, 1.0, 0.0).astype(jnp.bfloat16)
    counted = lax.dot_general(placing[...], good, (((1,), (1,)), ((), ())), preferred_element_type=jnp.float32)
    factor[...] = jnp.minimum(counted, 1.0) / jnp.maximum(counted, 1.0)
    wide_group = cols // GROUPS
    for q in range(GROUPS):
        spread[:, q * wide_group : (q + 1) * wide_group] = jnp.broadcast_to(
            counted[:, q : q + 1], (rows, wide_group)
        ).astype(jnp.bfloat16)


def cover(got, row_count, cols):
    sources = got.shape[0]
    slots = sources * SLOT_CAP
    vmem = pl.BlockSpec(memory_space=pltpu.VMEM)
    return pl.pallas_call(
        cover_kernel,
        out_shape=(
            jax.ShapeDtypeStruct((VISITS * row_count, slots * BLOCK_ROWS), jnp.bfloat16),
            jax.ShapeDtypeStruct((VISITS * row_count, cols), jnp.bfloat16),
            jax.ShapeDtypeStruct((VISITS * row_count, 128), jnp.float32),
        ),
        in_specs=[pl.BlockSpec(memory_space=pl.ANY)],
        out_specs=(vmem, vmem, vmem),
        scratch_shapes=[pltpu.VMEM((sources, META_ROWS, 128), jnp.bfloat16), pltpu.SemaphoreType.DMA],
        compiler_params=params(24),
        name="coverage",
    )(got)


def column_kernel(padded, table, out):
    for k in range(out.shape[2] // 128):
        window = padded[:, k * 128 : k * 128 + 256]
        result = jnp.dot(window, table[...], preferred_element_type=jnp.float32)
        for j in range(NPOW):
            out[j, :, k * 128 : (k + 1) * 128] = result[:, j * 128 : (j + 1) * 128].astype(jnp.bfloat16)


def column_pass(padded, taps, cols):
    rows = padded.shape[0]
    vmem = pl.BlockSpec(memory_space=pltpu.VMEM)
    table = jnp.asarray(column_table(taps).astype(ml_dtypes.bfloat16))
    return pl.pallas_call(
        column_kernel,
        out_shape=jax.ShapeDtypeStruct((NPOW, rows, cols), jnp.bfloat16),
        in_specs=[vmem, vmem],
        out_specs=vmem,
        compiler_params=params(24),
        name="column_pass",
    )(padded, table)


GRAM_ROWS = 240


def gram_kernel(images, table, count, out, stage, acc):
    cols = images.shape[2]
    rows = count.shape[0] // VISITS
    chunk = stage.shape[1]
    ones = jnp.ones((8, chunk), jnp.float32)
    blank = jnp.zeros((8, chunk), jnp.float32)
    acc[...] = jnp.zeros_like(acc)

    def tile(step, carry):
        first = pl.multiple_of(step * TILE, TILE)
        for k in range(cols // chunk):
            lanes = slice(k * chunk, (k + 1) * chunk)
            at = 0
            for j in range(NPOW):
                size = TILE * (NPOW - j)
                window = images[j, pl.ds(first, SPAN), lanes]
                stage[at : at + size, :] = jnp.dot(
                    table[at : at + size, :], window, preferred_element_type=jnp.float32
                )
                at += size
            for pair in range(TILE // 16):
                seen = [
                    jnp.minimum(
                        count[pl.ds(pl.multiple_of(v * rows + first + pair * 16, 16), 16), lanes].astype(jnp.float32), 1.0
                    )
                    for v in range(VISITS)
                ]
                for half in range(2):
                    cb = pair * 2 + half
                    pieces = []
                    at = 0
                    for j in range(NPOW):
                        size = 8 * (NPOW - j)
                        pieces.append(stage[at + cb * size : at + (cb + 1) * size, :])
                        at += TILE * (NPOW - j)
                    basis = jnp.concatenate(pieces + [ones, blank], axis=0)
                    scaled = []
                    for v in range(VISITS):
                        w = seen[v][half * 8 : half * 8 + 8]
                        scaled.append(
                            (basis.reshape(GRAM_ROWS // 8, 8, chunk) * w[None])
                            .reshape(GRAM_ROWS, chunk)
                            .astype(jnp.bfloat16)
                        )
                    acc[...] += lax.dot_general(
                        jnp.concatenate(scaled, axis=0),
                        basis.astype(jnp.bfloat16),
                        (((1,), (1,)), ((), ())),
                        preferred_element_type=jnp.float32,
                    )
        return carry

    lax.fori_loop(0, rows // TILE, tile, 0)
    row_id = lax.broadcasted_iota(jnp.int32, (GRAM_ROWS, GRAM_ROWS), 0)
    lane_id = lax.broadcasted_iota(jnp.int32, (GRAM_ROWS, GRAM_ROWS), 1)
    same = (row_id % 8) == (lane_id % 8)
    gather = jnp.where(
        lax.broadcasted_iota(jnp.int32, (GRAM_ROWS, 128), 0) // 8
        == lax.broadcasted_iota(jnp.int32, (GRAM_ROWS, 128), 1),
        1.0,
        0.0,
    )
    for v in range(VISITS):
        kept = jnp.where(same, acc[v * GRAM_ROWS : (v + 1) * GRAM_ROWS, :], 0.0)
        kept = jnp.sum(kept.reshape(GRAM_ROWS // 8, 8, GRAM_ROWS), axis=1)
        full = jnp.dot(kept, gather, precision=lax.Precision.HIGHEST, preferred_element_type=jnp.float32)
        out[v] = full[:TERMS, :TERMS]


def gram(images, count, taps):
    vmem = pl.BlockSpec(memory_space=pltpu.VMEM)
    table = jnp.asarray(row_table(taps).astype(ml_dtypes.bfloat16))
    return pl.pallas_call(
        gram_kernel,
        out_shape=jax.ShapeDtypeStruct((VISITS, TERMS, TERMS), jnp.float32),
        in_specs=[vmem, vmem, vmem],
        out_specs=vmem,
        scratch_shapes=[
            pltpu.VMEM((BASIS_COUNT * TILE, 1024), jnp.float32),
            pltpu.VMEM((VISITS * GRAM_ROWS, GRAM_ROWS), jnp.float32),
        ],
        compiler_params=params(28),
        name="normal_matrix",
    )(images, table, count)


ONES_ROWS = 16
PLACE_CHUNK = 512


def scale_rows(summed, factor, first, group):
    rows = summed.shape[0]
    spread = jnp.concatenate(
        [
            jnp.broadcast_to(factor[:, first + q : first + q + 1], (rows, group))
            for q in range(summed.shape[1] // group)
        ],
        axis=1,
    )
    return (summed * spread).astype(jnp.bfloat16)


def correlate(value, images, lanes, rows, partial):
    chunk = value.shape[1]
    ones = jnp.ones((ONES_ROWS, chunk), jnp.bfloat16)
    for t in range(rows // TILE):
        left = jnp.concatenate(
            [value[v * rows + t * TILE : v * rows + (t + 1) * TILE, :] for v in range(VISITS)], axis=0
        )
        right = images[:, t * TILE : t * TILE + SPAN, lanes].reshape(NPOW * SPAN, chunk)
        right = jnp.concatenate([right, ones], axis=0)
        product = lax.dot_general(left, right, (((1,), (1,)), ((), ())), preferred_element_type=jnp.float32)
        partial = product if partial is None else partial + product
    return partial


def early_kernel(got, placing, factor, images, science, acc, buf, sem):
    rows = science.shape[1]
    copy = pltpu.make_async_copy(got.at[:, pl.ds(0, buf.shape[1]), :], buf, sem)
    copy.start()
    copy.wait()
    columns = []
    for q in range(FIRST):
        ranks = [
            buf[:, (r * FIRST + q) * BLOCK_ROWS : (r * FIRST + q + 1) * BLOCK_ROWS, :] for r in range(SLOT_CAP)
        ]
        columns.append(jnp.stack(ranks, axis=1).reshape(-1, 128))
    right = jnp.concatenate(columns, axis=1)
    summed = jnp.dot(placing[...], right, preferred_element_type=jnp.float32)
    value = scale_rows(summed, factor, 0, 128)
    for v in range(VISITS):
        science[v, :, :] = value[v * rows : (v + 1) * rows, :]
    acc[...] = correlate(value, images, slice(0, FIRST * 128), rows, None)


def place_early(got, placing, factor, images, row_count):
    sources = got.shape[0]
    vmem = pl.BlockSpec(memory_space=pltpu.VMEM)
    return pl.pallas_call(
        early_kernel,
        out_shape=(
            jax.ShapeDtypeStruct((VISITS, row_count, FIRST * 128), jnp.bfloat16),
            jax.ShapeDtypeStruct((VISITS * TILE, NPOW * SPAN + ONES_ROWS), jnp.float32),
        ),
        in_specs=[pl.BlockSpec(memory_space=pl.ANY), vmem, vmem, vmem],
        out_specs=(vmem, vmem),
        scratch_shapes=[
            pltpu.VMEM((sources, SLOT_CAP * FIRST * BLOCK_ROWS, 128), jnp.bfloat16),
            pltpu.SemaphoreType.DMA,
        ],
        compiler_params=params(28),
        name="place_first_groups",
    )(got, placing, factor, images)


def place_kernel(got, placing, factor_hbm, source, table_hbm, before_hbm, science, sums, images, buf, acc, factor, table, before, sem_got, sem_img, sem_small):
    rows = science.shape[1]
    cols = science.shape[2]
    skip = source.shape[2] - cols
    chunk = PLACE_CHUNK
    group = source.shape[2] // GROUPS
    small = pltpu.make_async_copy(factor_hbm, factor, sem_small.at[0])
    small.start()
    later = [
        pltpu.make_async_copy(before_hbm, before, sem_small.at[1]),
        pltpu.make_async_copy(table_hbm, table, sem_small.at[2]),
    ]
    rest = pltpu.make_async_copy(source.at[:, :, pl.ds(0, skip)], images.at[:, :, pl.ds(0, skip)], sem_img.at[cols // chunk])
    copies = []
    for c in range(cols // chunk):
        lanes = slice(c * chunk, (c + 1) * chunk)
        late = slice(skip + c * chunk, skip + (c + 1) * chunk)
        copies.append(
            (
                pltpu.make_async_copy(got.at[:, :, lanes], buf.at[:, :, lanes], sem_got.at[c]),
                pltpu.make_async_copy(source.at[:, :, late], images.at[:, :, late], sem_img.at[c]),
            )
        )
    for pair in copies[:2]:
        for item in pair:
            item.start()
    partial = None
    for c in range(cols // chunk):
        lanes = slice(c * chunk, (c + 1) * chunk)
        late = slice(skip + c * chunk, skip + (c + 1) * chunk)
        copies[c][0].wait()
        if c + 2 < len(copies):
            copies[c + 2][0].start()
        summed = jnp.dot(placing[...], buf[:, :, lanes].reshape(-1, chunk), preferred_element_type=jnp.float32)
        if c == 0:
            small.wait()
            for item in later:
                item.start()
        value = scale_rows(summed, factor, (skip + c * chunk) // group, group)
        for v in range(VISITS):
            science[v, :, lanes] = value[v * rows : (v + 1) * rows, :]
        copies[c][1].wait()
        if c + 2 < len(copies):
            copies[c + 2][1].start()
        if c == len(copies) - 2:
            rest.start()
        partial = correlate(value, images, late, rows, partial)
    for item in later:
        item.wait()
    acc[...] = partial + before[...]
    row_id = lax.broadcasted_iota(jnp.int32, (32, 128), 0)
    lane_id = lax.broadcasted_iota(jnp.int32, (32, 128), 1)
    result = jnp.zeros((32, 128), jnp.float32)
    for v in range(VISITS):
        parts = []
        for j in range(NPOW):
            cross = acc[v * TILE : (v + 1) * TILE, j * SPAN : (j + 1) * SPAN]
            for i in range(NPOW - j):
                parts.append(jnp.sum(cross * table[i], axis=0, keepdims=True))
        parts.append(jnp.zeros((32 - BASIS_COUNT, SPAN), jnp.float32))
        item = jnp.sum(jnp.concatenate(parts, axis=0), axis=1, keepdims=True)
        flat = jnp.sum(acc[v * TILE : (v + 1) * TILE, NPOW * SPAN : NPOW * SPAN + 1], axis=0, keepdims=True)
        item = jnp.where(row_id == BASIS_COUNT, flat, item)
        result = result + jnp.where(lane_id == v, item, 0.0)
    sums[...] = result
    rest.wait()


def place(got, placing, factor, images, bands, before, row_count):
    slots, _, cols = got.shape
    table = jnp.asarray(bands)
    vmem = pl.BlockSpec(memory_space=pltpu.VMEM)
    hbm = pl.BlockSpec(memory_space=pltpu.HBM)
    return pl.pallas_call(
        place_kernel,
        out_shape=(
            jax.ShapeDtypeStruct((VISITS, row_count, cols), jnp.bfloat16),
            jax.ShapeDtypeStruct((32, 128), jnp.float32),
            jax.ShapeDtypeStruct(images.shape, jnp.bfloat16),
        ),
        in_specs=[hbm, vmem, hbm, hbm, hbm, hbm],
        out_specs=(vmem, vmem, vmem),
        scratch_shapes=[
            pltpu.VMEM(got.shape, jnp.bfloat16),
            pltpu.VMEM((VISITS * TILE, NPOW * SPAN + ONES_ROWS), jnp.float32),
            pltpu.VMEM(factor.shape, jnp.float32),
            pltpu.VMEM(table.shape, jnp.float32),
            pltpu.VMEM(before.shape, jnp.float32),
            pltpu.SemaphoreType.DMA((cols // PLACE_CHUNK,)),
            pltpu.SemaphoreType.DMA((cols // PLACE_CHUNK + 1,)),
            pltpu.SemaphoreType.DMA((3,)),
        ],
        compiler_params=params(40),
        name="place_and_correlate",
    )(
        pltpu.with_memory_space_constraint(got, pltpu.HBM),
        placing,
        pltpu.with_memory_space_constraint(factor, pltpu.HBM),
        pltpu.with_memory_space_constraint(images, pltpu.HBM),
        pltpu.with_memory_space_constraint(table, pltpu.HBM),
        pltpu.with_memory_space_constraint(before, pltpu.HBM),
    )


def model_kernel(sums, inverse, table, images, early, science, count, out, coeffs, wide, narrow, buf, sem):
    rows = science.shape[1]
    skip = early.shape[2]
    cols = skip + science.shape[2]
    chunk = 256
    rhs = sums[0:32, :]
    for k in range(1, sums.shape[0] // 32):
        rhs = rhs + sums[k * 32 : (k + 1) * 32, :]
    level = []
    for v in range(VISITS):
        row = jnp.sum(inverse[v] * rhs[:, v : v + 1], axis=0, keepdims=True)
        coeffs[v : v + 1, :] = row[:, :TERMS]
        level.append(row[:, BASIS_COUNT : BASIS_COUNT + 1])
        index = 0
        for j in range(NPOW):
            kernel = jnp.zeros((TILE, SPAN), jnp.float32)
            for i in range(NPOW - j):
                kernel = kernel + row[:, index : index + 1] * table[i]
                index += 1
            wide[v * TILE : (v + 1) * TILE, j * SPAN : (j + 1) * SPAN] = kernel
    narrow[...] = wide[...].astype(jnp.bfloat16)
    copies = []
    for c in range(cols // chunk):
        lanes = slice(c * chunk, (c + 1) * chunk)
        for t in range(rows // TILE):
            right = images[:, t * TILE : t * TILE + SPAN, lanes].reshape(NPOW * SPAN, chunk)
            model = jnp.dot(narrow[...], right, preferred_element_type=jnp.float32)
            for v in range(VISITS):
                at = slice(t * TILE, (t + 1) * TILE)
                full = model[v * TILE : (v + 1) * TILE, :] + level[v]
                seen = count[v * rows + t * TILE : v * rows + (t + 1) * TILE, lanes]
                weight = jnp.minimum(seen.astype(jnp.float32), 1.0)
                if (c + 1) * chunk <= skip:
                    seen = early[v, at, lanes]
                else:
                    seen = science[v, at, c * chunk - skip : (c + 1) * chunk - skip]
                buf[v, at, lanes] = (seen.astype(jnp.float32) - weight * full).astype(jnp.bfloat16)
        copies.append(pltpu.make_async_copy(buf.at[:, :, lanes], out.at[:, :, lanes], sem.at[c]))
        copies[-1].start()
    for item in copies:
        item.wait()


def model(sums, inverse, images, early, science, count, bands):
    _, rows, cols = science.shape
    cols = cols + early.shape[2]
    table = jnp.asarray(bands)
    vmem = pl.BlockSpec(memory_space=pltpu.VMEM)
    return pl.pallas_call(
        model_kernel,
        out_shape=(
            pltpu.HBM((VISITS, rows, cols), jnp.bfloat16),
            jax.ShapeDtypeStruct((VISITS, TERMS), jnp.float32),
        ),
        in_specs=[vmem] * 7,
        out_specs=(pl.BlockSpec(memory_space=pltpu.HBM), vmem),
        scratch_shapes=[
            pltpu.VMEM((VISITS * TILE, NPOW * SPAN), jnp.float32),
            pltpu.VMEM((VISITS * TILE, NPOW * SPAN), jnp.bfloat16),
            pltpu.VMEM((VISITS, rows, cols), jnp.bfloat16),
            pltpu.SemaphoreType.DMA((cols // 256,)),
        ],
        compiler_params=params(28),
        name="model_and_difference",
    )(sums, inverse, table, images, early, science, count)


def inverse_of(matrix):
    eye = jnp.broadcast_to(jnp.eye(TERMS, dtype=jnp.float32), matrix.shape)
    lower = jnp.linalg.cholesky(matrix)
    half = jax.scipy.linalg.solve_triangular(lower, eye, lower=True)
    return jnp.einsum("vkb,vkc->vbc", half, half, precision=lax.Precision.HIGHEST)


def halo(rows):
    count = lax.axis_size("visit")
    up = [(i, i + 1) for i in range(count - 1)]
    down = [(i + 1, i) for i in range(count - 1)]
    above = lax.ppermute(rows[-MARGIN:], "visit", up)
    below = lax.ppermute(rows[:MARGIN], "visit", down)
    return above, below


def body(template, blocks, dest, offset, visit_id, badmask):
    row_count = template.shape[1]
    cols = template.shape[2]
    axes = ("patch", "visit")
    sources = lax.axis_size("patch") * lax.axis_size("visit")
    slots = sources * SLOT_CAP
    taps = taps_table()
    bands = row_bands(taps)

    flags = badmask.T
    send_first = pack_first(dest, offset, visit_id, flags, blocks, sources, row_count)
    send_first, rows = lax.optimization_barrier((send_first, template[0]))
    got_first = lax.all_to_all(send_first, axes, split_axis=0, concat_axis=0, tiled=True)
    send = pack(dest, flags, blocks, slots)
    above, below = halo(rows)
    tall = jnp.concatenate([above, rows, below], axis=0)
    padded = jnp.pad(tall, ((0, 0), (HALF_TAPS, 128 - HALF_TAPS)))
    images = column_pass(padded, taps, cols)
    send, got_first, images = lax.optimization_barrier((send, got_first, images))
    got = lax.all_to_all(send, axes, split_axis=0, concat_axis=0, tiled=True)

    placing, count, factor = cover(got_first, row_count, cols)

    early, before = place_early(got_first, placing, factor, images, row_count)
    images, before = lax.optimization_barrier((images, before))
    shares = lax.all_gather(gram(images, count, taps), "visit", axis=0, tiled=False)
    normal = jnp.sum(shares, axis=0)
    inverse = jnp.pad(inverse_of(normal), ((0, 0), (0, 32 - TERMS), (0, 128 - TERMS)))

    science, sums, images = place(got, placing, factor, images, bands, before, row_count)
    sums = lax.all_gather(sums, "visit", axis=0, tiled=True)
    difference, coeffs = model(sums, inverse, images, early, science, count, bands)
    return (difference[:, None], coeffs[:, None])


def solution(mesh):
    in_specs = (
        P("patch", "visit", None),
        P(("patch", "visit"), None, None),
        P(("patch", "visit")),
        P(("patch", "visit")),
        P(("patch", "visit")),
        P(("patch", "visit"), None),
    )
    out_specs = (P(None, "patch", "visit", None), P(None, "patch", None))
    return jax.shard_map(body, mesh=mesh, in_specs=in_specs, out_specs=out_specs, check_vma=False)
```
